256 devices in a mesh: grp: 2 (over core), seq: 32 (over y, z), head: 4 (over x).
Axes of the slice: x: 4, y: 4, z: 8, core: 2. Of those that a mesh axis runs over, the one named last changes fastest.
Arguments:
- queries: bfloat16 [16384, 8192], P('seq', ('grp', 'head')), may hold values from -140 to 140
- key_rows: bfloat16 [16384, 1024], P('seq', ('grp', 'head')), may hold values from -6 to 6
- values: bfloat16 [16384, 1024], P('seq', ('grp', 'head')), may hold values from -6 to 6
- out_grad: bfloat16 [16384, 8192], P('seq', ('grp', 'head')), may hold values from -6 to 6
- teacher_window: bfloat16 [128, 3, 64, 128, 128], P('seq', None, ('grp', 'head')), may hold values from -16 to 250
- teacher_global: bfloat16 [128, 2, 64, 128, 128], P('seq', None, ('grp', 'head')), may hold values from -16 to 250
- global_picks: int32 [128, 2], P('seq'), may hold values from -1 to 3, as said below
- mix_weight: float32 [16384], P('seq'), may hold values from 0.05 to 0.95
Outputs:
- query_grad: bfloat16 [16384, 8192], P('seq', ('grp', 'head'))
- key_grad: bfloat16 [16384, 1024], P('seq', ('grp', 'head'))
- value_grad: bfloat16 [16384, 1024], P('seq', ('grp', 'head'))
- row_loss: float32 [16384], P('seq')
The draws below stay inside these ranges and needn't reach their ends.
Inputs may be any that keep to these rules, and one draw needn't show every extreme that they name: `global_picks`: in each row the non-negative entries are distinct, and an entry of query block b is below b - 2.
All inputs are finite; a program needn't handle non-finite values.
Results may differ from the reference program's by a relative error of at most 0.005.
Values may be sent and summed in bfloat16 or wider, within the bound.
A program may use at most 128 MiB of HBM per device.

```python
import math
import jax
import jax.numpy as jnp
from jax import lax

H = 64
KVH = 8
E = 128
BLK = 128
WIN = 3
NGLOB = 4
GSEL = 2
NQB = 128
TOKENS = 16384


def shared_keys(key):
    base = jax.random.normal(jax.random.fold_in(key, 101), (TOKENS, KVH * E), jnp.float32)
    return jnp.clip(base, -6.0, 6.0)


def draw_key_rows(key, part):
    return shared_keys(key).astype(jnp.bfloat16)


def draw_queries(key, part):
    base = jnp.clip(jax.random.normal(jax.random.fold_in(key, 102), (TOKENS, H * E), jnp.float32), -6.0, 6.0)
    return base.astype(jnp.bfloat16)


def draw_teacher_window(key, part):
    shape = (NQB, WIN, H, BLK, BLK)
    base = jnp.clip(2.0 * jax.random.normal(jax.random.fold_in(key, 111), shape, jnp.float32), -16.0, 16.0)
    return base.astype(jnp.bfloat16)


def draw_teacher_global(key, part):
    shape = (NQB, GSEL, H, BLK, BLK)
    base = jnp.clip(2.0 * jax.random.normal(jax.random.fold_in(key, 121), shape, jnp.float32), -16.0, 16.0)
    return base.astype(jnp.bfloat16)


def draw_global_picks(key, part):
    row_keys = jax.random.split(jax.random.fold_in(key, 201), NQB)
    orders = jax.vmap(lambda row_key: jax.random.permutation(row_key, NGLOB))(row_keys).astype(jnp.int32)[:, :GSEL]
    keeping = jax.random.randint(jax.random.fold_in(key, 202), (NQB, GSEL), 0, 4) > 0
    limits = jnp.arange(NQB, dtype=jnp.int32)[:, None] - (WIN - 1)
    return jnp.where(keeping & (orders < limits), orders, -1).astype(jnp.int32)


def block_scale(own_key, dims, shards, smallest, top_value):
    gain = 1.0
    for dim, shards_of in shards:
        steps = jax.random.uniform(jax.random.fold_in(jax.random.fold_in(own_key, 6), dim), (shards_of,), jnp.float32, smallest / len(shards), top_value / len(shards))
        gain = gain * jnp.repeat(jnp.exp(steps), dims[dim] // shards_of).reshape((-1,) + (1,) * (len(dims) - 1 - dim))
    return gain


def noise(stream_key, extent, spread, limit, cuts=(), kind=jnp.bfloat16):
    values = spread * jax.random.normal(stream_key, extent, jnp.float32)
    if cuts:
        values = values * block_scale(stream_key, extent, cuts, -0.22, 0.18)
    return jnp.clip(values, -limit, limit).astype(kind)


def setup_inputs(seed: int = 0) -> dict:
    key_list = jax.random.split(jax.random.key(seed), 9)
    queries = draw_queries(jax.random.fold_in(key_list[8], 71), 0)
    key_rows = draw_key_rows(jax.random.fold_in(key_list[8], 71), 0)
    values = noise(key_list[2], (TOKENS, KVH * E), 1.0, 6.0, ((0, 32), (1, 8)))
    out_grad = noise(key_list[3], (TOKENS, H * E), 1.0, 6.0, ((0, 32), (1, 8)))
    teacher_window = draw_teacher_window(jax.random.fold_in(key_list[8], 71), 0)
    teacher_global = draw_teacher_global(jax.random.fold_in(key_list[8], 71), 0)
    global_picks = draw_global_picks(jax.random.fold_in(key_list[8], 71), 0)
    mix_weight = jnp.clip(0.05 + 0.9 * jax.random.uniform(key_list[7], (TOKENS,), jnp.float32) ** block_scale(key_list[7], (TOKENS,), ((0, 32),), -0.2, 0.2), 0.05, 0.95)
    return dict(queries=queries, key_rows=key_rows, values=values, out_grad=out_grad, teacher_window=teacher_window, teacher_global=teacher_global, global_picks=global_picks, mix_weight=mix_weight)


def block_terms(query_tiles, key_cat, value_cat, teacher_cat, live_slots, grad_tiles, weights, scale):
    hiprec = lax.Precision.HIGHEST
    nblk, rows, kv_heads, group, width = query_tiles.shape
    slots = key_cat.shape[1]
    query_f = query_tiles.astype(jnp.float32)
    key_f = key_cat.astype(jnp.float32)
    value_f = value_cat.astype(jnp.float32)
    grad_f = grad_tiles.astype(jnp.float32)
    scores = jnp.einsum('bqnge,bsjne->bsngqj', query_f, key_f, precision=hiprec) * scale
    causal = lax.broadcasted_iota(jnp.int32, (rows, rows), 1) <= lax.broadcasted_iota(jnp.int32, (rows, rows), 0)
    later_slot = jnp.arange(slots) > 0
    live = live_slots[:, :, None, None, None, None] & (causal[None, None, None, None] | later_slot[None, :, None, None, None, None])
    masked = jnp.where(live, scores, -1000000000.0)
    shifted = masked - lax.optimization_barrier(jnp.max(masked, axis=(1, 5), keepdims=True))
    expo = jnp.where(live, jnp.exp(shifted), 0.0)
    total = lax.optimization_barrier(jnp.sum(expo, axis=(1, 5), keepdims=True))
    student_p = expo / total
    student_logp = shifted - jnp.log(total)
    teacher_grouped = teacher_cat.reshape(nblk, slots, kv_heads, group, rows, rows)
    teacher = jnp.where(live, teacher_grouped.astype(jnp.float32), -1000000000.0)
    teacher_shift = teacher - lax.optimization_barrier(jnp.max(teacher, axis=(1, 5), keepdims=True))
    teacher_exp = jnp.where(live, jnp.exp(teacher_shift), 0.0)
    teacher_total = lax.optimization_barrier(jnp.sum(teacher_exp, axis=(1, 5), keepdims=True))
    teacher_p = teacher_exp / teacher_total
    teacher_logp = teacher_shift - jnp.log(teacher_total)
    forward_kl = lax.optimization_barrier(jnp.sum(jnp.where(live, teacher_p * (teacher_logp - student_logp), 0.0), axis=(1, 5), keepdims=True))
    reverse_kl = lax.optimization_barrier(jnp.sum(jnp.where(live, student_p * (student_logp - teacher_logp), 0.0), axis=(1, 5), keepdims=True))
    mixing = weights[:, None, None, None, :, None]
    row_terms = lax.optimization_barrier(jnp.sum(mixing * forward_kl + (1.0 - mixing) * reverse_kl, axis=(1, 2, 3, 5)))
    probs_low = student_p.astype(jnp.bfloat16)
    prob_grad = jnp.einsum('bqnge,bsjne->bsngqj', grad_f, value_f, precision=hiprec)
    delta = lax.optimization_barrier(jnp.sum(student_p * prob_grad, axis=(1, 5), keepdims=True))
    score_grad = jnp.where(live, mixing * (student_p - teacher_p) + (1.0 - mixing) * student_p * (student_logp - teacher_logp - reverse_kl) + student_p * (prob_grad - delta), 0.0) * scale
    score_low = score_grad.astype(jnp.bfloat16).astype(jnp.float32)
    query_part = jnp.einsum('bsngqj,bsjne->bqnge', score_low, key_f, precision=hiprec)
    key_part = jnp.einsum('bsngqj,bqnge->bsjne', score_low, query_f, precision=hiprec)
    value_part = jnp.einsum('bsngqj,bqnge->bsjne', probs_low.astype(jnp.float32), grad_f, precision=hiprec)
    return (query_part, key_part, value_part, row_terms)

def reference(queries, key_rows, values, out_grad, teacher_window, teacher_global, global_picks, mix_weight):
    scale = 1.0 / math.sqrt(E)
    group = H // KVH
    lead_rows = (WIN - 1) * BLK
    query_tiles = queries.reshape(NQB, BLK, KVH, group, E)
    grad_tiles = out_grad.reshape(NQB, BLK, KVH, group, E)
    weight_rows = mix_weight.reshape(NQB, BLK)
    pad_block = jnp.zeros((lead_rows, KVH * E), jnp.bfloat16)
    key_padded = jnp.concatenate([pad_block, key_rows], axis=0).reshape(-1, KVH, E)
    value_padded = jnp.concatenate([pad_block, values], axis=0).reshape(-1, KVH, E)
    key_global = key_rows[:NGLOB * BLK].reshape(NGLOB, BLK, KVH, E)
    value_global = values[:NGLOB * BLK].reshape(NGLOB, BLK, KVH, E)

    def one_block(carry, block_id):
        key_acc, value_acc, key_sink, value_sink = carry
        start = (block_id * BLK).astype(jnp.int32)
        key_window = lax.dynamic_slice_in_dim(key_padded, start, WIN * BLK, 0).reshape(WIN, BLK, KVH, E)[::-1]
        value_window = lax.dynamic_slice_in_dim(value_padded, start, WIN * BLK, 0).reshape(WIN, BLK, KVH, E)[::-1]
        picks_row = global_picks[block_id]
        safe_picks = jnp.maximum(picks_row, 0).astype(jnp.int32)
        key_cat = jnp.concatenate([key_window, jnp.take(key_global, safe_picks, axis=0)], axis=0)[None]
        value_cat = jnp.concatenate([value_window, jnp.take(value_global, safe_picks, axis=0)], axis=0)[None]
        window_tiles = jnp.stack([teacher_window[jnp.maximum(block_id - offset, 0).astype(jnp.int32), offset] for offset in range(WIN)])
        teacher_cat = jnp.concatenate([window_tiles, teacher_global[block_id]], axis=0)[None]
        live_window = block_id - jnp.arange(WIN, dtype=jnp.int32) >= 0
        live_slots = jnp.concatenate([live_window, picks_row >= 0])[None]
        query_part, key_part, value_part, row_terms = block_terms(query_tiles[block_id][None], key_cat, value_cat, teacher_cat, live_slots, grad_tiles[block_id][None], weight_rows[block_id][None], scale)
        key_win = key_part[0, :WIN][::-1].reshape(WIN * BLK, KVH, E)
        value_win = value_part[0, :WIN][::-1].reshape(WIN * BLK, KVH, E)
        key_acc = lax.dynamic_update_slice_in_dim(key_acc, lax.dynamic_slice_in_dim(key_acc, start, WIN * BLK, 0) + key_win, start, 0)
        value_acc = lax.dynamic_update_slice_in_dim(value_acc, lax.dynamic_slice_in_dim(value_acc, start, WIN * BLK, 0) + value_win, start, 0)
        onehot = (picks_row[:, None] == jnp.arange(NGLOB, dtype=jnp.int32)[None, :]).astype(jnp.float32)
        key_sink = key_sink + jnp.einsum('gn,gkhe->nkhe', onehot, key_part[0, WIN:], precision=lax.Precision.HIGHEST)
        value_sink = value_sink + jnp.einsum('gn,gkhe->nkhe', onehot, value_part[0, WIN:], precision=lax.Precision.HIGHEST)
        return ((key_acc, value_acc, key_sink, value_sink), (query_part[0], row_terms[0]))
    acc_zero = jnp.zeros((lead_rows + TOKENS, KVH, E), jnp.float32)
    sink_zero = jnp.zeros((NGLOB, BLK, KVH, E), jnp.float32)
    carry, outputs = lax.scan(one_block, (acc_zero, acc_zero, sink_zero, sink_zero), jnp.arange(NQB, dtype=jnp.int32))
    key_acc, value_acc, key_sink, value_sink = carry
    query_parts, loss_rows = outputs
    key_full = key_acc[lead_rows:].at[:NGLOB * BLK].add(key_sink.reshape(NGLOB * BLK, KVH, E))
    value_full = value_acc[lead_rows:].at[:NGLOB * BLK].add(value_sink.reshape(NGLOB * BLK, KVH, E))
    query_grad = query_parts.reshape(TOKENS, H * E).astype(jnp.bfloat16)
    key_grad = key_full.reshape(TOKENS, KVH * E).astype(jnp.bfloat16)
    value_grad = value_full.reshape(TOKENS, KVH * E).astype(jnp.bfloat16)
    return (query_grad, key_grad, value_grad, loss_rows.reshape(TOKENS))
```

```python
import functools
import math

import jax
import jax.numpy as jnp
from jax import lax
from jax.experimental import pallas as pl
from jax.experimental.pallas import tpu as pltpu
from jax.sharding import PartitionSpec as P

E = 128
BLK = 128
WIN = 3
NGLOB = 4
NB = 4
HEADS = 8
SLOTS = 5
ROWS = 16
LOG2E = math.log2(math.e)
LN2 = math.log(2.0)
SCALE = 1.0 / math.sqrt(E)
NEG = -1.0e30
MESH = pl.DeviceIdType.MESH
F32 = jnp.float32
BF16 = jnp.bfloat16
CHUNKS = 2 * NGLOB
LOCAL_TILES = [(c, d) for c in range(NB) for d in range(WIN) if c + d < NB]
CROSS = [(3, 2), (3, 1), (2, 2)]


def split_of(size):
    z = 1
    while size % z or size // z > z:
        z += 1
    return size // z, z


def kernel(
    nseq, ngrp, nhead,
    q_h, k_h, v_h, do_h, tw_h, tg_h, picks, mix_ref,
    qg_h, kgrad, vgrad, loss_out,
    q_v, do_v, tw_v, tg_v, th_v, k_v, v_v, glob, kc, vc,
    s_scr, dp_scr, sg_scr, p_scr, dkt, dvt, mixc, loss_scr, lbuf,
    acc_k, acc_v, sink, qg_v, sbuf, rbuf, hs, hr,
    lsem, hsend, hrecv, bsend, brecv, rsend, rrecv, gsend, grecv, lsend, lrecv, osem,
):
    ny, nz = split_of(nseq)
    seq = lax.axis_index("seq")
    grp = lax.axis_index("grp")
    head = lax.axis_index("head")
    y = seq // nz
    z = seq % nz
    zhalf, yhalf = nz // 2, ny // 2
    z_up, z_dn = lax.rem(z + 1, nz), lax.rem(z + nz - 1, nz)
    y_up, y_dn = lax.rem(y + 1, ny), lax.rem(y + ny - 1, ny)
    dev_zu, dev_zd = y * nz + z_up, y * nz + z_dn
    dev_yu, dev_yd = y_up * nz + z, y_dn * nz + z
    nxt, prv = lax.rem(seq + 1, nseq), lax.rem(seq + nseq - 1, nseq)
    kid_zu = (z < zhalf) if nz > 1 else (z < 0)
    kid_zd = ((z == 0) | (z > zhalf + 1)) if nz > 2 else (z < 0)
    kid_yu = (y < yhalf) if ny > 1 else (y < 0)
    kid_yd = ((y == 0) | (y > yhalf + 1)) if ny > 2 else (y < 0)
    kids = [
        [(0, dev_zu, kid_zu), (1, dev_zd, kid_zd), (2, dev_yu, kid_yu & (z == 0)), (3, dev_yd, kid_yd & (z == 0))],
        [(0, dev_zu, kid_zu & (y == 0)), (1, dev_zd, kid_zd & (y == 0)), (2, dev_yu, kid_yu), (3, dev_yd, kid_yd)],
    ]
    z_low = z <= zhalf
    y_low = y <= yhalf
    z_par = jnp.where(z_low, dev_zd, dev_zu)
    z_slot = jnp.where(z_low, 0, 1)
    y_par = jnp.where(y_low, dev_yd, dev_yu)
    y_slot = jnp.where(y_low, 2, 3)
    parents = [
        (jnp.where(z > 0, z_par, y_par), jnp.where(z > 0, z_slot, y_slot)),
        (jnp.where(y > 0, y_par, z_par), jnp.where(y > 0, y_slot, z_slot)),
    ]
    is_root = seq == 0

    loads = {}
    count = [0]

    def load(key, src, dst):
        copy = pltpu.make_async_copy(src, dst, lsem.at[count[0]])
        count[0] += 1
        copy.start()
        loads.setdefault(key, []).append(copy)

    load("kv", k_h, k_v.at[pl.ds(WIN - 1, NB)])
    load("kv", v_h, v_v.at[pl.ds(WIN - 1, NB)])
    for b in reversed(range(NB)):
        load(b, q_h.at[b], q_v.at[b])
        load(b, do_h.at[b], do_v.at[b])
        for c, d in LOCAL_TILES:
            if c + d == b:
                load(b, tw_h.at[c, d], tw_v.at[c, d])
        load(b, tg_h.at[b], tg_v.at[b])

    barrier = pltpu.get_barrier_semaphore()
    waits = 0
    for dev in (dev_zu, dev_zd, dev_yu, dev_yd, nxt, prv):
        pl.semaphore_signal(barrier, inc=1, device_id={"seq": dev}, device_id_type=MESH)
        waits += 1
    peers = []
    for off in range(1, ngrp * nhead):
        flat = lax.rem(grp * nhead + head + off, ngrp * nhead)
        peers.append((flat // nhead, flat % nhead))
    for pg, ph in peers:
        pl.semaphore_signal(barrier, inc=1, device_id={"grp": pg, "head": ph}, device_id_type=MESH)
        waits += 1
    pl.semaphore_wait(barrier, waits)

    def halo_copies():
        out = []
        ends = [
            (k_h.at[pl.ds(NB - WIN + 1, WIN - 1)], k_v.at[pl.ds(0, WIN - 1)]),
            (v_h.at[pl.ds(NB - WIN + 1, WIN - 1)], v_v.at[pl.ds(0, WIN - 1)]),
        ] + [(tw_h.at[c, d], th_v.at[i]) for i, (c, d) in enumerate(CROSS)]
        for i, (src, dst) in enumerate(ends):
            out.append(
                pltpu.make_async_remote_copy(
                    src, dst, hsend.at[i], hrecv.at[i], device_id={"seq": nxt}, device_id_type=MESH
                )
            )
        return out

    halo = halo_copies()

    @pl.when(seq < nseq - 1)
    def _():
        for copy in halo:
            copy.start()

    def bcast(c, slot, dev):
        return pltpu.make_async_remote_copy(
            glob.at[c], glob.at[c], bsend.at[slot, c], brecv.at[c],
            device_id={"seq": dev}, device_id_type=MESH,
        )

    @pl.when(is_root)
    def _():
        a = pltpu.make_async_copy(k_h, glob.at[pl.ds(0, NGLOB)], lsem.at[count[0]])
        b = pltpu.make_async_copy(v_h, glob.at[pl.ds(NGLOB, NGLOB)], lsem.at[count[0] + 1])
        a.start()
        b.start()
        k_v[pl.ds(0, WIN - 1)] = jnp.zeros((WIN - 1, BLK, E), BF16)
        v_v[pl.ds(0, WIN - 1)] = jnp.zeros((WIN - 1, BLK, E), BF16)
        th_v[...] = jnp.zeros_like(th_v)
        a.wait()
        b.wait()

    order = [0, 2, 1, 3, 4, 6, 5, 7]
    for c in order:
        tree = (c // 2) % 2

        @pl.when(jnp.logical_not(is_root))
        def _():
            bcast(c, 0, parents[tree][0]).wait_recv()

        for slot, dev, cond in kids[tree]:

            @pl.when(cond)
            def _():
                bcast(c, slot, dev).start()

    for b in range(NB):
        mixc[b] = jnp.broadcast_to(mix_ref[pl.ds(b, 1), :], (BLK, BLK)).T
    acc_k[...] = jnp.zeros_like(acc_k)
    acc_v[...] = jnp.zeros_like(acc_v)
    sink[...] = jnp.zeros_like(sink)

    for copy in loads["kv"]:
        copy.wait()

    col = lax.broadcasted_iota(jnp.int32, (ROWS, BLK), 1)
    row = lax.broadcasted_iota(jnp.int32, (ROWS, BLK), 0)
    dims_t = (((1,), (1,)), ((), ()))
    dims_c = (((0,), (0,)), ((), ()))

    def halo_wait(indices):
        @pl.when(seq > 0)
        def _():
            for i in indices:
                halo[i].wait_recv()

    def block(b):
        if b == 1:
            halo_wait([0, 1, 2])
        if b == 0:
            halo_wait([3, 4])
        for copy in loads[b]:
            copy.wait()
        for d in range(WIN):
            kc[pl.ds(d * BLK, BLK), :] = k_v[b + WIN - 1 - d]
            vc[pl.ds(d * BLK, BLK), :] = v_v[b + WIN - 1 - d]
        biases = [None] * SLOTS
        for d in range(1, WIN):
            if b < d:
                biases[d] = jnp.where(seq > 0, 0.0, NEG)
        for g in range(SLOTS - WIN):
            pick = picks[b, g]
            safe = jnp.maximum(pick, 0)
            kc[pl.ds((WIN + g) * BLK, BLK), :] = glob[safe]
            vc[pl.ds((WIN + g) * BLK, BLK), :] = glob[safe + NGLOB]
            biases[WIN + g] = jnp.where(pick >= 0, 0.0, NEG)
        tiles = []
        for d in range(WIN):
            if b >= d:
                tiles.append(tw_v.at[b - d, d])
            else:
                tiles.append(th_v.at[CROSS.index((NB + b - d, d))])
        for g in range(SLOTS - WIN):
            tiles.append(tg_v.at[b, g])
        dkt[...] = jnp.zeros_like(dkt)
        dvt[...] = jnp.zeros_like(dvt)
        loss_scr[...] = jnp.zeros_like(loss_scr)

        def pair(i, carry):
            h0 = 2 * i
            lanes = [pl.ds(pl.multiple_of((h0 + e) * E, E), E) for e in range(2)]
            q2 = jnp.concatenate([q_v[b, :, lanes[0]], q_v[b, :, lanes[1]]], axis=0)
            do2 = jnp.concatenate([do_v[b, :, lanes[0]], do_v[b, :, lanes[1]]], axis=0)
            keys = kc[...]
            s_scr[...] = lax.dot_general(q2, keys, dims_t, preferred_element_type=F32)
            dp_scr[...] = lax.dot_general(do2, vc[...], dims_t, preferred_element_type=F32)
            for n in range(2 * BLK // ROWS):
                e, r0 = n // (BLK // ROWS), (n % (BLK // ROWS)) * ROWS
                at = pl.ds(n * ROWS, ROWS)
                ss, ts = [], []
                for j in range(SLOTS):
                    s = s_scr[at, pl.ds(j * BLK, BLK)] * (SCALE * LOG2E)
                    t = tiles[j][h0 + e, pl.ds(r0, ROWS), :].astype(F32) * LOG2E
                    if j == 0:
                        live = col <= row + r0
                        s = jnp.where(live, s, NEG)
                        t = jnp.where(live, t, NEG)
                    elif biases[j] is not None:
                        s = s + biases[j]
                        t = t + biases[j]
                    ss.append(s)
                    ts.append(t)
                m_s = jnp.max(functools.reduce(jnp.maximum, ss), axis=1, keepdims=True)
                m_t = jnp.max(functools.reduce(jnp.maximum, ts), axis=1, keepdims=True)
                mix = mixc[b, pl.ds(r0, ROWS), :]
                other = (1.0 - mix) * LN2
                es, et, xs = [], [], []
                z_s = z_t = f_u = r_u = x_u = None
                for j in range(SLOTS):
                    sp = ss[j] - m_s
                    tp = ts[j] - m_t
                    e_s = jnp.exp2(sp)
                    e_t = jnp.exp2(tp)
                    u = sp - tp
                    x = other * u + dp_scr[at, pl.ds(j * BLK, BLK)]
                    terms = (e_s, e_t, e_t * u, e_s * u, e_s * x)
                    if j == 0:
                        z_s, z_t, f_u, r_u, x_u = terms
                    else:
                        z_s, z_t, f_u, r_u, x_u = (
                            z_s + terms[0], z_t + terms[1], f_u + terms[2], r_u + terms[3], x_u + terms[4],
                        )
                    es.append(e_s)
                    et.append(e_t)
                    xs.append(x)
                z_s, z_t, f_u, r_u, x_u = (
                    jnp.sum(v, axis=1, keepdims=True) for v in (z_s, z_t, f_u, r_u, x_u)
                )
                i_s = 1.0 / z_s
                i_t = 1.0 / z_t
                c = jnp.log(z_t) - jnp.log(z_s)
                fkl = -(f_u * i_t * LN2 + c)
                rkl = r_u * i_s * LN2 + c
                loss_scr[pl.ds(r0, ROWS), :] += mix * fkl + (1.0 - mix) * rkl
                shift = mix - x_u * i_s
                t_fac = mix * i_t
                for j in range(SLOTS):
                    p = es[j] * i_s
                    p_scr[at, pl.ds(j * BLK, BLK)] = p.astype(BF16)
                    sg_scr[at, pl.ds(j * BLK, BLK)] = (p * (xs[j] + shift) - t_fac * et[j]).astype(BF16)
            sg = sg_scr[...]
            qg = (jnp.dot(sg, keys, preferred_element_type=F32) * SCALE).astype(BF16)
            qg_v[b, :, lanes[0]] = qg[:BLK]
            qg_v[b, :, lanes[1]] = qg[BLK:]
            dkt[...] += lax.dot_general(q2, sg, dims_c, preferred_element_type=F32)
            dvt[...] += lax.dot_general(do2, p_scr[...], dims_c, preferred_element_type=F32)
            return carry

        lax.fori_loop(0, HEADS // 2, pair, 0)
        pltpu.make_async_copy(qg_v.at[b], qg_h.at[b], osem.at[b]).start()
        for d in range(WIN):
            acc_k[b + WIN - 1 - d] += dkt[:, pl.ds(d * BLK, BLK)] * SCALE
            acc_v[b + WIN - 1 - d] += dvt[:, pl.ds(d * BLK, BLK)]
        for g in range(SLOTS - WIN):
            pick = picks[b, g]
            for n in range(NGLOB):
                hit = jnp.where(pick == n, 1.0, 0.0)
                sink[n] += dkt[:, pl.ds((WIN + g) * BLK, BLK)] * (hit * SCALE)
                sink[NGLOB + n] += dvt[:, pl.ds((WIN + g) * BLK, BLK)] * hit
        lbuf[0, pl.ds(b, 1), :] = loss_scr[...].T[0:1, :]

    for b in reversed(range(NB)):
        block(b)

    hs[0] = acc_k[pl.ds(0, WIN - 1)].astype(BF16)
    hs[1] = acc_v[pl.ds(0, WIN - 1)].astype(BF16)
    back = pltpu.make_async_remote_copy(
        hs, hr, gsend.at[0], grecv.at[0], device_id={"seq": prv}, device_id_type=MESH
    )

    loss_copies = []
    for n, (pg, ph) in enumerate(peers):
        copy = pltpu.make_async_remote_copy(
            lbuf.at[0], lbuf.at[n + 1], lsend.at[n], lrecv.at[n],
            device_id={"grp": pg, "head": ph}, device_id_type=MESH,
        )
        copy.start()
        loss_copies.append(copy)

    def up(c, dev, slot):
        return pltpu.make_async_remote_copy(
            sbuf.at[c], rbuf.at[slot, c], rsend.at[c], rrecv.at[slot, c],
            device_id={"seq": dev}, device_id_type=MESH,
        )

    for c in order:
        tree = (c // 2) % 2
        for slot, dev, cond in kids[tree]:

            @pl.when(cond)
            def _():
                up(c, dev, slot).wait_recv()
                sink[c] += rbuf[slot, c].astype(F32)

        @pl.when(jnp.logical_not(is_root))
        def _():
            sbuf[c] = sink[c].astype(BF16)
            dev, slot = parents[tree]
            up(c, dev, slot).start()

        if c == order[0]:

            @pl.when(seq > 0)
            def _():
                back.start()

    @pl.when(seq < nseq - 1)
    def _():
        back.wait_recv()
        acc_k[pl.ds(NB, WIN - 1)] += hr[0].astype(F32)
        acc_v[pl.ds(NB, WIN - 1)] += hr[1].astype(F32)

    @pl.when(is_root)
    def _():
        acc_k[pl.ds(WIN - 1, NB)] += sink[pl.ds(0, NGLOB)]
        acc_v[pl.ds(WIN - 1, NB)] += sink[pl.ds(NGLOB, NGLOB)]

    for b in range(NB):
        kgrad[b] = acc_k[b + WIN - 1].T.astype(BF16)
        vgrad[b] = acc_v[b + WIN - 1].T.astype(BF16)

    total = lbuf[0]
    for n, copy in enumerate(loss_copies):
        copy.wait_recv()
        total = total + lbuf[n + 1]
    loss_out[...] = total

    for b in range(NB):
        pltpu.make_async_copy(qg_v.at[b], qg_h.at[b], osem.at[b]).wait()
    for copy in loss_copies:
        copy.wait_send()

    @pl.when(seq > 0)
    def _():
        back.wait_send()

    @pl.when(seq < nseq - 1)
    def _():
        for copy in halo:
            copy.wait_send()

    for c in order:
        tree = (c // 2) % 2
        for slot, dev, cond in kids[tree]:

            @pl.when(cond)
            def _():
                bcast(c, slot, dev).wait_send()

        @pl.when(jnp.logical_not(is_root))
        def _():
            dev, slot = parents[tree]
            up(c, dev, slot).wait_send()


def local(queries, key_rows, values, out_grad, teacher_window, teacher_global, global_picks, mix_weight):
    nseq, ngrp, nhead = (lax.axis_size(a) for a in ("seq", "grp", "head"))
    width = HEADS * E
    hbm = pl.BlockSpec(memory_space=pl.ANY)
    vmem = pl.BlockSpec(memory_space=pltpu.VMEM)
    smem = pl.BlockSpec(memory_space=pltpu.SMEM)
    dma = pltpu.SemaphoreType.DMA
    npeer = max(ngrp * nhead - 1, 1)
    tile = (BLK, E)
    scratch = [
        pltpu.VMEM((NB, BLK, width), BF16),
        pltpu.VMEM((NB, BLK, width), BF16),
        pltpu.VMEM((NB, WIN, HEADS, BLK, BLK), BF16),
        pltpu.VMEM((NB, SLOTS - WIN, HEADS, BLK, BLK), BF16),
        pltpu.VMEM((len(CROSS), HEADS, BLK, BLK), BF16),
        pltpu.VMEM((NB + WIN - 1,) + tile, BF16),
        pltpu.VMEM((NB + WIN - 1,) + tile, BF16),
        pltpu.VMEM((CHUNKS,) + tile, BF16),
        pltpu.VMEM((SLOTS * BLK, E), BF16),
        pltpu.VMEM((SLOTS * BLK, E), BF16),
        pltpu.VMEM((2 * BLK, SLOTS * BLK), F32),
        pltpu.VMEM((2 * BLK, SLOTS * BLK), F32),
        pltpu.VMEM((2 * BLK, SLOTS * BLK), BF16),
        pltpu.VMEM((2 * BLK, SLOTS * BLK), BF16),
        pltpu.VMEM((E, SLOTS * BLK), F32),
        pltpu.VMEM((E, SLOTS * BLK), F32),
        pltpu.VMEM((NB, BLK, BLK), F32),
        pltpu.VMEM((BLK, BLK), F32),
        pltpu.VMEM((npeer + 1, NB, BLK), F32),
        pltpu.VMEM((NB + WIN - 1,) + tile, F32),
        pltpu.VMEM((NB + WIN - 1,) + tile, F32),
        pltpu.VMEM((CHUNKS,) + tile, F32),
        pltpu.VMEM((NB, BLK, width), BF16),
        pltpu.VMEM((CHUNKS,) + tile, BF16),
        pltpu.VMEM((4, CHUNKS) + tile, BF16),
        pltpu.VMEM((2, WIN - 1) + tile, BF16),
        pltpu.VMEM((2, WIN - 1) + tile, BF16),
        dma((32,)),
        dma((5,)),
        dma((5,)),
        dma((4, CHUNKS)),
        dma((CHUNKS,)),
        dma((CHUNKS,)),
        dma((4, CHUNKS)),
        dma((1,)),
        dma((1,)),
        dma((npeer,)),
        dma((npeer,)),
        dma((NB,)),
    ]
    out = pl.pallas_call(
        functools.partial(kernel, nseq, ngrp, nhead),
        out_shape=(
            jax.ShapeDtypeStruct((NB, BLK, width), BF16),
            jax.ShapeDtypeStruct((NB, BLK, E), BF16),
            jax.ShapeDtypeStruct((NB, BLK, E), BF16),
            jax.ShapeDtypeStruct((NB, BLK), F32),
        ),
        in_specs=[hbm] * 6 + [smem, vmem],
        out_specs=(hbm, vmem, vmem, vmem),
        scratch_shapes=scratch,
        compiler_params=pltpu.CompilerParams(
            collective_id=0, has_side_effects=True, vmem_limit_bytes=48 * 1024 * 1024
        ),
        name="distill_backward",
    )(
        queries.reshape(NB, BLK, width),
        key_rows.reshape(NB, BLK, E),
        values.reshape(NB, BLK, E),
        out_grad.reshape(NB, BLK, width),
        teacher_window,
        teacher_global,
        global_picks,
        mix_weight.reshape(NB, BLK),
    )
    query_grad, key_grad, value_grad, row_loss = out
    return (
        query_grad.reshape(NB * BLK, width),
        key_grad.reshape(NB * BLK, E),
        value_grad.reshape(NB * BLK, E),
        row_loss.reshape(NB * BLK),
    )


def solution(mesh):
    placed = (
        P("seq", ("grp", "head")),
        P("seq", ("grp", "head")),
        P("seq", ("grp", "head")),
        P("seq", ("grp", "head")),
        P("seq", None, ("grp", "head"), None, None),
        P("seq", None, ("grp", "head"), None, None),
        P("seq", None),
        P("seq"),
    )
    return jax.shard_map(
        local,
        mesh=mesh,
        in_specs=placed,
        out_specs=(
            P("seq", ("grp", "head")),
            P("seq", ("grp", "head")),
            P("seq", ("grp", "head")),
            P("seq"),
        ),
        check_vma=False,
    )
```

```python
import functools
import math

import jax
import jax.numpy as jnp
from jax import lax
from jax.experimental import pallas as pl
from jax.experimental.pallas import tpu as pltpu
from jax.sharding import PartitionSpec as P

E = 128
BLK = 128
WIN = 3
NGLOB = 4
NB = 4
HEADS = 8
SLOTS = 5
ROWS = 16
LOG2E = math.log2(math.e)
LN2 = math.log(2.0)
SCALE = 1.0 / math.sqrt(E)
NEG = -1.0e30
MESH = pl.DeviceIdType.MESH
F32 = jnp.float32
BF16 = jnp.bfloat16
CHUNKS = 2 * NGLOB
LOCAL_TILES = [(c, d) for c in range(NB) for d in range(WIN) if c + d < NB]
HALO_A = [0, 1, 2]
HALO_B = [3, 4]
CROSS = [(3, 2), (3, 1), (2, 2)]


def kernel(
    nseq, ngrp, nhead,
    q_h, k_h, v_h, do_h, tw_h, tg_h, picks, mix_h,
    qg_h, kgrad, vgrad, loss_out,
    q_v, do_v, tw_v, tg_v, th_v, k_v, v_v, glob, glob_kv, kc, vc,
    s_scr, dp_scr, sg_scr, p_scr, dkt, dvt, mix_ref, mixc, loss_scr, lbuf,
    acc_k, acc_v, sink, qg_v, sbuf, rbuf, tsum, hs, hr,
    lsem, hsend, hrecv, bsend, brecv, rsend, rrecv, gsend, grecv, lsend, lrecv, osem,
):
    seq = lax.axis_index("seq")
    grp = lax.axis_index("grp")
    head = lax.axis_index("head")
    piece = CHUNKS * BLK // nseq
    others = [lax.rem(seq + off, nseq) for off in range(1, nseq)]
    nxt, prv = others[0], others[-1]

    def rows_of(dev):
        return pl.ds(pl.multiple_of(dev * piece, piece), piece)

    def total_wait(ref, sem):
        part = ref.at[pl.ds(0, (nseq - 1) * piece)]
        pltpu.make_async_copy(part, part, sem).wait()

    is_root = seq == 0

    loads = {}
    count = [0]

    def load(key, src, dst):
        copy = pltpu.make_async_copy(src, dst, lsem.at[count[0]])
        count[0] += 1
        copy.start()
        loads.setdefault(key, []).append(copy)

    load("mix", mix_h, mix_ref)
    load("kv", k_h, k_v.at[pl.ds((WIN - 1) * BLK, NB * BLK)])
    load("kv", v_h, v_v.at[pl.ds((WIN - 1) * BLK, NB * BLK)])
    for b in reversed(range(NB)):
        load(b, q_h.at[b], q_v.at[b])
        load(b, do_h.at[b], do_v.at[b])
        for c, d in LOCAL_TILES:
            if c + d == b:
                load(b, tw_h.at[c, d], tw_v.at[c, d])
        load(b, tg_h.at[b], tg_v.at[b])

    barrier = pltpu.get_barrier_semaphore()
    waits = 2
    for dev in (nxt, prv):
        pl.semaphore_signal(barrier, inc=1, device_id={"seq": dev}, device_id_type=MESH)

    @pl.when(jnp.logical_not(is_root))
    def _():
        pl.semaphore_signal(barrier, inc=1, device_id={"seq": 0}, device_id_type=MESH)

    peers = []
    for off in range(1, ngrp * nhead):
        flat = lax.rem(grp * nhead + head + off, ngrp * nhead)
        peers.append((flat // nhead, flat % nhead))
    for pg, ph in peers:
        pl.semaphore_signal(barrier, inc=1, device_id={"grp": pg, "head": ph}, device_id_type=MESH)
        waits += 1

    @pl.when(jnp.logical_not(is_root))
    def _():
        pl.semaphore_wait(barrier, waits)

    @pl.when(is_root)
    def _():
        pl.semaphore_wait(barrier, waits + nseq - 1)

    def halo_copies():
        out = []
        ends = [
            (k_h.at[pl.ds((NB - WIN + 1) * BLK, (WIN - 1) * BLK)], k_v.at[pl.ds(0, (WIN - 1) * BLK)]),
            (v_h.at[pl.ds((NB - WIN + 1) * BLK, (WIN - 1) * BLK)], v_v.at[pl.ds(0, (WIN - 1) * BLK)]),
        ] + [(tw_h.at[c, d], th_v.at[i]) for i, (c, d) in enumerate(CROSS)]
        for i, (src, dst) in enumerate(ends):
            out.append(
                pltpu.make_async_remote_copy(
                    src, dst, hsend.at[i], hrecv.at[i], device_id={"seq": nxt}, device_id_type=MESH
                )
            )
        return out

    halo = halo_copies()

    def halo_start(indices):
        @pl.when(seq < nseq - 1)
        def _():
            for i in indices:
                halo[i].start()

    @pl.when(is_root)
    def _():
        half = nseq // 2
        for dev in range(nseq):
            src = (k_h if dev < half else v_h).at[pl.ds((dev % half) * piece, piece)]
            dst = glob.at[pl.ds(dev * piece, piece)]
            if dev:
                pltpu.make_async_remote_copy(
                    src, dst, bsend.at[0], brecv.at[0], device_id={"seq": dev}, device_id_type=MESH
                ).start()
            else:
                pltpu.make_async_copy(src, dst, brecv.at[0]).start()
        k_v[pl.ds(0, (WIN - 1) * BLK)] = jnp.zeros(((WIN - 1) * BLK, E), BF16)
        v_v[pl.ds(0, (WIN - 1) * BLK)] = jnp.zeros(((WIN - 1) * BLK, E), BF16)
        th_v[...] = jnp.zeros_like(th_v)

    halo_start(HALO_A)
    mine = glob.at[rows_of(seq)]
    pltpu.make_async_copy(mine, mine, brecv.at[0]).wait()
    for dev in others:
        pltpu.make_async_remote_copy(
            mine, mine, bsend.at[1], brecv.at[1], device_id={"seq": dev}, device_id_type=MESH
        ).start()
    halo_start(HALO_B)

    for copy in loads["mix"]:
        copy.wait()
    for b in range(NB):
        mixc[b] = jnp.broadcast_to(mix_ref[pl.ds(b, 1), :], (BLK, BLK)).T
    total_wait(glob, brecv.at[1])
    for n in range(CHUNKS):
        glob_kv[n] = glob[pl.ds(n * BLK, BLK), :]
    acc_k[...] = jnp.zeros_like(acc_k)
    acc_v[...] = jnp.zeros_like(acc_v)
    sink[...] = jnp.zeros_like(sink)

    for copy in loads["kv"]:
        copy.wait()

    col = lax.broadcasted_iota(jnp.int32, (ROWS, BLK), 1)
    row = lax.broadcasted_iota(jnp.int32, (ROWS, BLK), 0)
    dims_t = (((1,), (1,)), ((), ()))
    dims_c = (((0,), (0,)), ((), ()))

    def halo_wait(indices):
        @pl.when(seq > 0)
        def _():
            for i in indices:
                halo[i].wait_recv()

    def block(b):
        if b == 1:
            halo_wait([0, 1, 2])
        if b == 0:
            halo_wait([3, 4])
        for copy in loads[b]:
            copy.wait()
        for d in range(WIN):
            kc[pl.ds(d * BLK, BLK), :] = k_v[pl.ds((b + WIN - 1 - d) * BLK, BLK), :]
            vc[pl.ds(d * BLK, BLK), :] = v_v[pl.ds((b + WIN - 1 - d) * BLK, BLK), :]
        biases = [None] * SLOTS
        for d in range(1, WIN):
            if b < d:
                biases[d] = jnp.where(seq > 0, 0.0, NEG)
        for g in range(SLOTS - WIN):
            pick = picks[g, b]
            safe = jnp.maximum(pick, 0)
            kc[pl.ds((WIN + g) * BLK, BLK), :] = glob_kv[safe]
            vc[pl.ds((WIN + g) * BLK, BLK), :] = glob_kv[safe + NGLOB]
            biases[WIN + g] = jnp.where(pick >= 0, 0.0, NEG)
        tiles = []
        for d in range(WIN):
            if b >= d:
                tiles.append(tw_v.at[b - d, d])
            else:
                tiles.append(th_v.at[CROSS.index((NB + b - d, d))])
        for g in range(SLOTS - WIN):
            tiles.append(tg_v.at[b, g])
        dkt[...] = jnp.zeros_like(dkt)
        dvt[...] = jnp.zeros_like(dvt)
        loss_scr[...] = jnp.zeros_like(loss_scr)

        def pair(i, carry):
            h0 = 2 * i
            lanes = [pl.ds(pl.multiple_of((h0 + e) * E, E), E) for e in range(2)]
            q2 = jnp.concatenate([q_v[b, :, lanes[0]], q_v[b, :, lanes[1]]], axis=0)
            do2 = jnp.concatenate([do_v[b, :, lanes[0]], do_v[b, :, lanes[1]]], axis=0)
            keys = kc[...]
            s_scr[...] = lax.dot_general(q2, keys, dims_t, preferred_element_type=F32)
            dp_scr[...] = lax.dot_general(do2, vc[...], dims_t, preferred_element_type=F32)
            for n in range(2 * BLK // ROWS):
                e, r0 = n // (BLK // ROWS), (n % (BLK // ROWS)) * ROWS
                at = pl.ds(n * ROWS, ROWS)
                ss, ts = [], []
                for j in range(SLOTS):
                    s = s_scr[at, pl.ds(j * BLK, BLK)] * (SCALE * LOG2E)
                    t = tiles[j][h0 + e, pl.ds(r0, ROWS), :].astype(F32) * LOG2E
                    if j == 0:
                        live = col <= row + r0
                        s = jnp.where(live, s, NEG)
                        t = jnp.where(live, t, NEG)
                    elif biases[j] is not None:
                        s = s + biases[j]
                        t = t + biases[j]
                    ss.append(s)
                    ts.append(t)
                m_s = jnp.max(functools.reduce(jnp.maximum, ss), axis=1, keepdims=True)
                m_t = jnp.max(functools.reduce(jnp.maximum, ts), axis=1, keepdims=True)
                mix = mixc[b, pl.ds(r0, ROWS), :]
                other = (1.0 - mix) * LN2
                es, et, xs = [], [], []
                z_s = z_t = f_u = r_u = x_u = None
                for j in range(SLOTS):
                    sp = ss[j] - m_s
                    tp = ts[j] - m_t
                    e_s = jnp.exp2(sp)
                    e_t = jnp.exp2(tp)
                    u = sp - tp
                    x = other * u + dp_scr[at, pl.ds(j * BLK, BLK)]
                    terms = (e_s, e_t, e_t * u, e_s * u, e_s * x)
                    if j == 0:
                        z_s, z_t, f_u, r_u, x_u = terms
                    else:
                        z_s, z_t, f_u, r_u, x_u = (
                            z_s + terms[0], z_t + terms[1], f_u + terms[2], r_u + terms[3], x_u + terms[4],
                        )
                    es.append(e_s)
                    et.append(e_t)
                    xs.append(x)
                z_s, z_t, f_u, r_u, x_u = (
                    jnp.sum(v, axis=1, keepdims=True) for v in (z_s, z_t, f_u, r_u, x_u)
                )
                i_s = 1.0 / z_s
                i_t = 1.0 / z_t
                c = jnp.log(z_t) - jnp.log(z_s)
                fkl = -(f_u * i_t * LN2 + c)
                rkl = r_u * i_s * LN2 + c
                loss_scr[pl.ds(r0, ROWS), :] += mix * fkl + (1.0 - mix) * rkl
                shift = mix - x_u * i_s
                t_fac = mix * i_t
                for j in range(SLOTS):
                    p = es[j] * i_s
                    p_scr[at, pl.ds(j * BLK, BLK)] = p.astype(BF16)
                    sg_scr[at, pl.ds(j * BLK, BLK)] = (p * (xs[j] + shift) - t_fac * et[j]).astype(BF16)
            sg = sg_scr[...]
            qg = (jnp.dot(sg, keys, preferred_element_type=F32) * SCALE).astype(BF16)
            qg_v[b, :, lanes[0]] = qg[:BLK]
            qg_v[b, :, lanes[1]] = qg[BLK:]
            dkt[...] += lax.dot_general(q2, sg, dims_c, preferred_element_type=F32)
            dvt[...] += lax.dot_general(do2, p_scr[...], dims_c, preferred_element_type=F32)
            return carry

        lax.fori_loop(0, HEADS // 2, pair, 0)
        pltpu.make_async_copy(qg_v.at[b], qg_h.at[b], osem.at[b]).start()
        for d in range(WIN):
            acc_k[b + WIN - 1 - d] += dkt[:, pl.ds(d * BLK, BLK)] * SCALE
            acc_v[b + WIN - 1 - d] += dvt[:, pl.ds(d * BLK, BLK)]
        for g in range(SLOTS - WIN):
            pick = picks[g, b]
            for n in range(NGLOB):
                hit = jnp.where(pick == n, 1.0, 0.0)
                sink[pl.ds(n * BLK, BLK), :] += dkt[:, pl.ds((WIN + g) * BLK, BLK)] * (hit * SCALE)
                sink[pl.ds((NGLOB + n) * BLK, BLK), :] += dvt[:, pl.ds((WIN + g) * BLK, BLK)] * hit
        lbuf[0, pl.ds(b, 1), :] = loss_scr[...].T[0:1, :]

    for b in reversed(range(NB)):
        block(b)

    sbuf[...] = sink[...].astype(BF16)
    hs[0] = acc_k[pl.ds(0, WIN - 1)].astype(BF16)
    hs[1] = acc_v[pl.ds(0, WIN - 1)].astype(BF16)
    for n, dev in enumerate(others):
        pltpu.make_async_remote_copy(
            sbuf.at[rows_of(dev)], rbuf.at[pl.ds(n * piece, piece)], rsend.at[0], rrecv.at[0],
            device_id={"seq": dev}, device_id_type=MESH,
        ).start()

    back = pltpu.make_async_remote_copy(
        hs, hr, gsend.at[0], grecv.at[0], device_id={"seq": prv}, device_id_type=MESH
    )

    @pl.when(seq > 0)
    def _():
        back.start()

    loss_copies = []
    for n, (pg, ph) in enumerate(peers):
        copy = pltpu.make_async_remote_copy(
            lbuf.at[0], lbuf.at[n + 1], lsend.at[n], lrecv.at[n],
            device_id={"grp": pg, "head": ph}, device_id_type=MESH,
        )
        copy.start()
        loss_copies.append(copy)

    total_wait(rbuf, rrecv.at[0])
    summed = sink[rows_of(seq), :]
    for n in range(nseq - 1):
        summed = summed + rbuf[pl.ds(n * piece, piece), :].astype(F32)
    tsum[rows_of(seq), :] = summed.astype(BF16)
    give = pltpu.make_async_remote_copy(
        tsum.at[rows_of(seq)], tsum.at[rows_of(seq)], rsend.at[1], rrecv.at[1],
        device_id={"seq": 0}, device_id_type=MESH,
    )

    @pl.when(jnp.logical_not(is_root))
    def _():
        give.start()

    @pl.when(seq < nseq - 1)
    def _():
        back.wait_recv()
        acc_k[pl.ds(NB, WIN - 1)] += hr[0].astype(F32)
        acc_v[pl.ds(NB, WIN - 1)] += hr[1].astype(F32)

    @pl.when(is_root)
    def _():
        total_wait(tsum, rrecv.at[1])
        for n in range(NGLOB):
            acc_k[WIN - 1 + n] += tsum[pl.ds(n * BLK, BLK), :].astype(F32)
            acc_v[WIN - 1 + n] += tsum[pl.ds((NGLOB + n) * BLK, BLK), :].astype(F32)

    for b in range(NB):
        kgrad[b] = acc_k[b + WIN - 1].T.astype(BF16)
        vgrad[b] = acc_v[b + WIN - 1].T.astype(BF16)

    total = lbuf[0]
    for n, copy in enumerate(loss_copies):
        copy.wait_recv()
        total = total + lbuf[n + 1]
    loss_out[...] = total

    for b in range(NB):
        pltpu.make_async_copy(qg_v.at[b], qg_h.at[b], osem.at[b]).wait()
    for copy in loss_copies:
        copy.wait_send()

    @pl.when(seq > 0)
    def _():
        back.wait_send()

    @pl.when(seq < nseq - 1)
    def _():
        for copy in halo:
            copy.wait_send()

    total_wait(glob, bsend.at[1])
    total_wait(sbuf, rsend.at[0])

    @pl.when(is_root)
    def _():
        total_wait(glob, bsend.at[0])

    @pl.when(jnp.logical_not(is_root))
    def _():
        give.wait_send()


def local(queries, key_rows, values, out_grad, teacher_window, teacher_global, global_picks, mix_weight):
    nseq, ngrp, nhead = (lax.axis_size(a) for a in ("seq", "grp", "head"))
    width = HEADS * E
    hbm = pl.BlockSpec(memory_space=pltpu.HBM)
    vmem = pl.BlockSpec(memory_space=pltpu.VMEM)
    dma = pltpu.SemaphoreType.DMA
    npeer = max(ngrp * nhead - 1, 1)
    tile = (BLK, E)
    scratch = [
        pltpu.VMEM((NB, BLK, width), BF16),
        pltpu.VMEM((NB, BLK, width), BF16),
        pltpu.VMEM((NB, WIN, HEADS, BLK, BLK), BF16),
        pltpu.VMEM((NB, SLOTS - WIN, HEADS, BLK, BLK), BF16),
        pltpu.VMEM((len(CROSS), HEADS, BLK, BLK), BF16),
        pltpu.VMEM(((NB + WIN - 1) * BLK, E), BF16),
        pltpu.VMEM(((NB + WIN - 1) * BLK, E), BF16),
        pltpu.VMEM((CHUNKS * BLK, E), BF16),
        pltpu.VMEM((CHUNKS,) + tile, BF16),
        pltpu.VMEM((SLOTS * BLK, E), BF16),
        pltpu.VMEM((SLOTS * BLK, E), BF16),
        pltpu.VMEM((2 * BLK, SLOTS * BLK), F32),
        pltpu.VMEM((2 * BLK, SLOTS * BLK), F32),
        pltpu.VMEM((2 * BLK, SLOTS * BLK), BF16),
        pltpu.VMEM((2 * BLK, SLOTS * BLK), BF16),
        pltpu.VMEM((E, SLOTS * BLK), F32),
        pltpu.VMEM((E, SLOTS * BLK), F32),
        pltpu.VMEM((NB, BLK), F32),
        pltpu.VMEM((NB, BLK, BLK), F32),
        pltpu.VMEM((BLK, BLK), F32),
        pltpu.VMEM((npeer + 1, NB, BLK), F32),
        pltpu.VMEM((NB + WIN - 1,) + tile, F32),
        pltpu.VMEM((NB + WIN - 1,) + tile, F32),
        pltpu.VMEM((CHUNKS * BLK, E), F32),
        pltpu.VMEM((NB, BLK, width), BF16),
        pltpu.VMEM((CHUNKS * BLK, E), BF16),
        pltpu.VMEM((CHUNKS * BLK, E), BF16),
        pltpu.VMEM((CHUNKS * BLK, E), BF16),
        pltpu.VMEM((2, WIN - 1) + tile, BF16),
        pltpu.VMEM((2, WIN - 1) + tile, BF16),
        dma((32,)),
        dma((5,)),
        dma((5,)),
        dma((2,)),
        dma((2,)),
        dma((2,)),
        dma((2,)),
        dma((1,)),
        dma((1,)),
        dma((npeer,)),
        dma((npeer,)),
        dma((NB,)),
    ]
    out = pl.pallas_call(
        functools.partial(kernel, nseq, ngrp, nhead),
        out_shape=(
            jax.ShapeDtypeStruct((NB, BLK, width), BF16),
            jax.ShapeDtypeStruct((NB, BLK, E), BF16),
            jax.ShapeDtypeStruct((NB, BLK, E), BF16),
            jax.ShapeDtypeStruct((NB, BLK), F32),
        ),
        in_specs=[hbm] * 6 + [pl.BlockSpec(memory_space=pltpu.SMEM), hbm],
        out_specs=(hbm, vmem, vmem, vmem),
        scratch_shapes=scratch,
        compiler_params=pltpu.CompilerParams(
            collective_id=0, has_side_effects=True, vmem_limit_bytes=48 * 1024 * 1024
        ),
        name="distill_backward",
    )(
        *(
            pltpu.with_memory_space_constraint(x, pltpu.HBM)
            for x in (
                queries.reshape(NB, BLK, width),
                key_rows,
                values,
                out_grad.reshape(NB, BLK, width),
                teacher_window,
                teacher_global,
            )
        ),
        global_picks.T,
        pltpu.with_memory_space_constraint(mix_weight.reshape(NB, BLK), pltpu.HBM),
    )
    query_grad, key_grad, value_grad, row_loss = out
    return (
        query_grad.reshape(NB * BLK, width),
        key_grad.reshape(NB * BLK, E),
        value_grad.reshape(NB * BLK, E),
        row_loss.reshape(NB * BLK),
    )


def solution(mesh):
    placed = (
        P("seq", ("grp", "head")),
        P("seq", ("grp", "head")),
        P("seq", ("grp", "head")),
        P("seq", ("grp", "head")),
        P("seq", None, ("grp", "head"), None, None),
        P("seq", None, ("grp", "head"), None, None),
        P("seq", None),
        P("seq"),
    )
    return jax.shard_map(
        local,
        mesh=mesh,
        in_specs=placed,
        out_specs=(
            P("seq", ("grp", "head")),
            P("seq", ("grp", "head")),
            P("seq", ("grp", "head")),
            P("seq"),
        ),
        check_vma=False,
    )
```

```python
import functools
import math

import jax
import jax.numpy as jnp
from jax import lax
from jax.experimental import pallas as pl
from jax.experimental.pallas import tpu as pltpu
from jax.sharding import PartitionSpec as P

E = 128
BLK = 128
WIN = 3
NGLOB = 4
NB = 4
HEADS = 8
SLOTS = 5
ROWS = 16
LOG2E = math.log2(math.e)
LN2 = math.log(2.0)
SCALE = 1.0 / math.sqrt(E)
NEG = -1.0e30
MESH = pl.DeviceIdType.MESH
F32 = jnp.float32
BF16 = jnp.bfloat16
CHUNKS = 2 * NGLOB
LOCAL_TILES = [(c, d) for c in range(NB) for d in range(WIN) if c + d < NB]
HALO_A = [0, 1]
HALO_B = [2, 3, 4]
UNROLL = 4
CROSS = [(3, 2), (3, 1), (2, 2)]


def kernel(
    nseq, ngrp, nhead,
    q_h, k_h, v_h, do_h, tw_h, tg_h, picks, mix_h,
    qg_h, kgrad, vgrad, loss_out,
    q_v, do_v, tw_v, tg_v, th_v, k_v, v_v, glob, glob_kv, kc, vc,
    s_scr, dp_scr, sg_scr, p_scr, dkt, dvt, mix_ref, mixc, loss_scr, lbuf,
    acc_k, acc_v, sink, qg_v, sbuf, rbuf, tsum, hs, hr,
    lsem, hsend, hrecv, bsend, brecv, rsend, rrecv, gsend, grecv, lsend, lrecv, osem,
):
    seq = lax.axis_index("seq")
    grp = lax.axis_index("grp")
    head = lax.axis_index("head")
    piece = CHUNKS * BLK // nseq
    others = [lax.rem(seq + off, nseq) for off in range(1, nseq)]
    nxt, prv = others[0], others[-1]

    def rows_of(dev):
        return pl.ds(pl.multiple_of(dev * piece, piece), piece)

    def total_wait(ref, sem):
        part = ref.at[pl.ds(0, (nseq - 1) * piece)]
        pltpu.make_async_copy(part, part, sem).wait()

    is_root = seq == 0

    loads = {}
    count = [0]

    def load(key, src, dst):
        copy = pltpu.make_async_copy(src, dst, lsem.at[count[0]])
        count[0] += 1
        copy.start()
        loads.setdefault(key, []).append(copy)

    load("mix", mix_h, mix_ref)
    load("kv", k_h, k_v.at[pl.ds((WIN - 1) * BLK, NB * BLK)])
    load("kv", v_h, v_v.at[pl.ds((WIN - 1) * BLK, NB * BLK)])
    for b in reversed(range(NB)):
        load(b, q_h.at[b], q_v.at[b])
        load(b, do_h.at[b], do_v.at[b])
        for c, d in LOCAL_TILES:
            if c + d == b:
                load(b, tw_h.at[c, d], tw_v.at[c, d])
        load(b, tg_h.at[b], tg_v.at[b])

    barrier = pltpu.get_barrier_semaphore()
    waits = 2
    for dev in (nxt, prv):
        pl.semaphore_signal(barrier, inc=1, device_id={"seq": dev}, device_id_type=MESH)

    @pl.when(jnp.logical_not(is_root))
    def _():
        pl.semaphore_signal(barrier, inc=1, device_id={"seq": 0}, device_id_type=MESH)

    peers = []
    for off in range(1, ngrp * nhead):
        flat = lax.rem(grp * nhead + head + off, ngrp * nhead)
        peers.append((flat // nhead, flat % nhead))
    for pg, ph in peers:
        pl.semaphore_signal(barrier, inc=1, device_id={"grp": pg, "head": ph}, device_id_type=MESH)
        waits += 1

    @pl.when(jnp.logical_not(is_root))
    def _():
        pl.semaphore_wait(barrier, waits)

    @pl.when(is_root)
    def _():
        pl.semaphore_wait(barrier, waits + nseq - 1)

    def halo_copies():
        out = []
        ends = [
            (k_h.at[pl.ds((NB - WIN + 1) * BLK, (WIN - 1) * BLK)], k_v.at[pl.ds(0, (WIN - 1) * BLK)]),
            (v_h.at[pl.ds((NB - WIN + 1) * BLK, (WIN - 1) * BLK)], v_v.at[pl.ds(0, (WIN - 1) * BLK)]),
        ] + [(tw_h.at[c, d], th_v.at[i]) for i, (c, d) in enumerate(CROSS)]
        for i, (src, dst) in enumerate(ends):
            out.append(
                pltpu.make_async_remote_copy(
                    src, dst, hsend.at[i], hrecv.at[i], device_id={"seq": nxt}, device_id_type=MESH
                )
            )
        return out

    halo = halo_copies()

    def halo_start(indices):
        @pl.when(seq < nseq - 1)
        def _():
            for i in indices:
                halo[i].start()

    @pl.when(is_root)
    def _():
        half = nseq // 2
        for dev in range(nseq):
            src = (k_h if dev < half else v_h).at[pl.ds((dev % half) * piece, piece)]
            dst = glob.at[pl.ds(dev * piece, piece)]
            if dev:
                pltpu.make_async_remote_copy(
                    src, dst, bsend.at[0], brecv.at[0], device_id={"seq": dev}, device_id_type=MESH
                ).start()
            else:
                pltpu.make_async_copy(src, dst, brecv.at[0]).start()
        k_v[pl.ds(0, (WIN - 1) * BLK)] = jnp.zeros(((WIN - 1) * BLK, E), BF16)
        v_v[pl.ds(0, (WIN - 1) * BLK)] = jnp.zeros(((WIN - 1) * BLK, E), BF16)
        th_v[...] = jnp.zeros_like(th_v)

    halo_start(HALO_A)
    mine = glob.at[rows_of(seq)]
    pltpu.make_async_copy(mine, mine, brecv.at[0]).wait()
    for dev in others:
        pltpu.make_async_remote_copy(
            mine, mine, bsend.at[1], brecv.at[1], device_id={"seq": dev}, device_id_type=MESH
        ).start()
    halo_start(HALO_B)

    for copy in loads["mix"]:
        copy.wait()
    for b in range(NB):
        mixc[b] = jnp.broadcast_to(mix_ref[pl.ds(b, 1), :], (BLK, BLK)).T
    total_wait(glob, brecv.at[1])
    for n in range(CHUNKS):
        glob_kv[n] = glob[pl.ds(n * BLK, BLK), :]
    acc_k[...] = jnp.zeros_like(acc_k)
    acc_v[...] = jnp.zeros_like(acc_v)
    sink[...] = jnp.zeros_like(sink)

    for copy in loads["kv"]:
        copy.wait()

    col = lax.broadcasted_iota(jnp.int32, (ROWS, BLK), 1)
    row = lax.broadcasted_iota(jnp.int32, (ROWS, BLK), 0)
    dims_t = (((1,), (1,)), ((), ()))
    dims_c = (((0,), (0,)), ((), ()))

    def halo_wait(indices):
        @pl.when(seq > 0)
        def _():
            for i in indices:
                halo[i].wait_recv()

    def block(b):
        if b == 1:
            halo_wait([0, 1, 2])
        if b == 0:
            halo_wait([3, 4])
        for copy in loads[b]:
            copy.wait()
        for d in range(WIN):
            kc[pl.ds(d * BLK, BLK), :] = k_v[pl.ds((b + WIN - 1 - d) * BLK, BLK), :]
            vc[pl.ds(d * BLK, BLK), :] = v_v[pl.ds((b + WIN - 1 - d) * BLK, BLK), :]
        biases = [None] * SLOTS
        for d in range(1, WIN):
            if b < d:
                biases[d] = jnp.where(seq > 0, 0.0, NEG)
        for g in range(SLOTS - WIN):
            pick = picks[g, b]
            safe = jnp.maximum(pick, 0)
            kc[pl.ds((WIN + g) * BLK, BLK), :] = glob_kv[safe]
            vc[pl.ds((WIN + g) * BLK, BLK), :] = glob_kv[safe + NGLOB]
            biases[WIN + g] = jnp.where(pick >= 0, 0.0, NEG)
        tiles = []
        for d in range(WIN):
            if b >= d:
                tiles.append(tw_v.at[b - d, d])
            else:
                tiles.append(th_v.at[CROSS.index((NB + b - d, d))])
        for g in range(SLOTS - WIN):
            tiles.append(tg_v.at[b, g])
        dkt[...] = jnp.zeros_like(dkt)
        dvt[...] = jnp.zeros_like(dvt)
        loss_scr[...] = jnp.zeros_like(loss_scr)

        def operands(i):
            h0 = 2 * i
            lanes = [pl.ds(pl.multiple_of((h0 + e) * E, E), E) for e in range(2)]
            q2 = jnp.concatenate([q_v[b, :, lanes[0]], q_v[b, :, lanes[1]]], axis=0)
            do2 = jnp.concatenate([do_v[b, :, lanes[0]], do_v[b, :, lanes[1]]], axis=0)
            return lanes, q2, do2

        def forward(i, k):
            lanes, q2, do2 = operands(i)
            s_scr[k] = lax.dot_general(q2, kc[...], dims_t, preferred_element_type=F32)
            dp_scr[k] = lax.dot_general(do2, vc[...], dims_t, preferred_element_type=F32)

        def middle(i, k):
            h0 = 2 * i
            for n in range(2 * BLK // ROWS):
                e, r0 = n // (BLK // ROWS), (n % (BLK // ROWS)) * ROWS
                at = pl.ds(n * ROWS, ROWS)
                ss, ts = [], []
                for j in range(SLOTS):
                    s = s_scr[k, at, pl.ds(j * BLK, BLK)] * (SCALE * LOG2E)
                    t = tiles[j][h0 + e, pl.ds(r0, ROWS), :].astype(F32) * LOG2E
                    if j == 0:
                        live = col <= row + r0
                        s = jnp.where(live, s, NEG)
                        t = jnp.where(live, t, NEG)
                    elif biases[j] is not None:
                        s = s + biases[j]
                        t = t + biases[j]
                    ss.append(s)
                    ts.append(t)
                m_s = jnp.max(functools.reduce(jnp.maximum, ss), axis=1, keepdims=True)
                m_t = jnp.max(functools.reduce(jnp.maximum, ts), axis=1, keepdims=True)
                mix = mixc[b, pl.ds(r0, ROWS), :]
                other = (1.0 - mix) * LN2
                es, et, xs = [], [], []
                z_s = z_t = f_u = r_u = x_u = None
                for j in range(SLOTS):
                    sp = ss[j] - m_s
                    tp = ts[j] - m_t
                    e_s = jnp.exp2(sp)
                    e_t = jnp.exp2(tp)
                    u = sp - tp
                    x = other * u + dp_scr[k, at, pl.ds(j * BLK, BLK)]
                    terms = (e_s, e_t, e_t * u, e_s * u, e_s * x)
                    if j == 0:
                        z_s, z_t, f_u, r_u, x_u = terms
                    else:
                        z_s, z_t, f_u, r_u, x_u = (
                            z_s + terms[0], z_t + terms[1], f_u + terms[2], r_u + terms[3], x_u + terms[4],
                        )
                    es.append(e_s)
                    et.append(e_t)
                    xs.append(x)
                z_s, z_t, f_u, r_u, x_u = (
                    jnp.sum(v, axis=1, keepdims=True) for v in (z_s, z_t, f_u, r_u, x_u)
                )
                i_s = 1.0 / z_s
                i_t = 1.0 / z_t
                c = jnp.log(z_t) - jnp.log(z_s)
                fkl = -(f_u * i_t * LN2 + c)
                rkl = r_u * i_s * LN2 + c
                loss_scr[pl.ds(r0, ROWS), :] += mix * fkl + (1.0 - mix) * rkl
                shift = mix - x_u * i_s
                t_fac = mix * i_t
                for j in range(SLOTS):
                    p = es[j] * i_s
                    p_scr[k, at, pl.ds(j * BLK, BLK)] = p.astype(BF16)
                    sg_scr[k, at, pl.ds(j * BLK, BLK)] = (p * (xs[j] + shift) - t_fac * et[j]).astype(BF16)

        def backward(i, k):
            lanes, q2, do2 = operands(i)
            sg = sg_scr[k]
            qg = (jnp.dot(sg, kc[...], preferred_element_type=F32) * SCALE).astype(BF16)
            qg_v[b, :, lanes[0]] = qg[:BLK]
            qg_v[b, :, lanes[1]] = qg[BLK:]
            dkt[...] += lax.dot_general(q2, sg, dims_c, preferred_element_type=F32)
            dvt[...] += lax.dot_general(do2, p_scr[k], dims_c, preferred_element_type=F32)

        def pairs(step, carry):
            base = step * UNROLL
            forward(base, 0)
            for k in range(UNROLL):
                if k + 1 < UNROLL:
                    forward(base + k + 1, k + 1)
                middle(base + k, k)
                if k:
                    backward(base + k - 1, k - 1)
            backward(base + UNROLL - 1, UNROLL - 1)
            return carry

        if UNROLL == HEADS // 2:
            pairs(0, 0)
        else:
            lax.fori_loop(0, HEADS // 2 // UNROLL, pairs, 0)
        pltpu.make_async_copy(qg_v.at[b], qg_h.at[b], osem.at[b]).start()
        for d in range(WIN):
            acc_k[b + WIN - 1 - d] += dkt[:, pl.ds(d * BLK, BLK)] * SCALE
            acc_v[b + WIN - 1 - d] += dvt[:, pl.ds(d * BLK, BLK)]
        for g in range(SLOTS - WIN):
            pick = picks[g, b]
            for n in range(NGLOB):
                hit = jnp.where(pick == n, 1.0, 0.0)
                sink[pl.ds(n * BLK, BLK), :] += dkt[:, pl.ds((WIN + g) * BLK, BLK)] * (hit * SCALE)
                sink[pl.ds((NGLOB + n) * BLK, BLK), :] += dvt[:, pl.ds((WIN + g) * BLK, BLK)] * hit
        lbuf[0, pl.ds(b, 1), :] = loss_scr[...].T[0:1, :]

    for b in reversed(range(NB)):
        block(b)

    sbuf[...] = sink[...].astype(BF16)
    hs[0] = acc_k[pl.ds(0, WIN - 1)].astype(BF16)
    hs[1] = acc_v[pl.ds(0, WIN - 1)].astype(BF16)
    for n, dev in enumerate(others):
        pltpu.make_async_remote_copy(
            sbuf.at[rows_of(dev)], rbuf.at[pl.ds(n * piece, piece)], rsend.at[0], rrecv.at[0],
            device_id={"seq": dev}, device_id_type=MESH,
        ).start()

    back = pltpu.make_async_remote_copy(
        hs, hr, gsend.at[0], grecv.at[0], device_id={"seq": prv}, device_id_type=MESH
    )

    @pl.when(seq > 0)
    def _():
        back.start()

    loss_copies = []
    for n, (pg, ph) in enumerate(peers):
        copy = pltpu.make_async_remote_copy(
            lbuf.at[0], lbuf.at[n + 1], lsend.at[n], lrecv.at[n],
            device_id={"grp": pg, "head": ph}, device_id_type=MESH,
        )
        copy.start()
        loss_copies.append(copy)

    total_wait(rbuf, rrecv.at[0])
    summed = sink[rows_of(seq), :]
    for n in range(nseq - 1):
        summed = summed + rbuf[pl.ds(n * piece, piece), :].astype(F32)
    tsum[rows_of(seq), :] = summed.astype(BF16)
    give = pltpu.make_async_remote_copy(
        tsum.at[rows_of(seq)], tsum.at[rows_of(seq)], rsend.at[1], rrecv.at[1],
        device_id={"seq": 0}, device_id_type=MESH,
    )

    @pl.when(jnp.logical_not(is_root))
    def _():
        give.start()

    @pl.when(seq < nseq - 1)
    def _():
        back.wait_recv()
        acc_k[pl.ds(NB, WIN - 1)] += hr[0].astype(F32)
        acc_v[pl.ds(NB, WIN - 1)] += hr[1].astype(F32)

    @pl.when(is_root)
    def _():
        total_wait(tsum, rrecv.at[1])
        for n in range(NGLOB):
            acc_k[WIN - 1 + n] += tsum[pl.ds(n * BLK, BLK), :].astype(F32)
            acc_v[WIN - 1 + n] += tsum[pl.ds((NGLOB + n) * BLK, BLK), :].astype(F32)

    for b in range(NB):
        kgrad[b] = acc_k[b + WIN - 1].T.astype(BF16)
        vgrad[b] = acc_v[b + WIN - 1].T.astype(BF16)

    total = lbuf[0]
    for n, copy in enumerate(loss_copies):
        copy.wait_recv()
        total = total + lbuf[n + 1]
    loss_out[...] = total

    for b in range(NB):
        pltpu.make_async_copy(qg_v.at[b], qg_h.at[b], osem.at[b]).wait()
    for copy in loss_copies:
        copy.wait_send()

    @pl.when(seq > 0)
    def _():
        back.wait_send()

    @pl.when(seq < nseq - 1)
    def _():
        for copy in halo:
            copy.wait_send()

    total_wait(glob, bsend.at[1])
    total_wait(sbuf, rsend.at[0])

    @pl.when(is_root)
    def _():
        total_wait(glob, bsend.at[0])

    @pl.when(jnp.logical_not(is_root))
    def _():
        give.wait_send()


def local(queries, key_rows, values, out_grad, teacher_window, teacher_global, global_picks, mix_weight):
    nseq, ngrp, nhead = (lax.axis_size(a) for a in ("seq", "grp", "head"))
    width = HEADS * E
    hbm = pl.BlockSpec(memory_space=pltpu.HBM)
    vmem = pl.BlockSpec(memory_space=pltpu.VMEM)
    dma = pltpu.SemaphoreType.DMA
    npeer = max(ngrp * nhead - 1, 1)
    tile = (BLK, E)
    scratch = [
        pltpu.VMEM((NB, BLK, width), BF16),
        pltpu.VMEM((NB, BLK, width), BF16),
        pltpu.VMEM((NB, WIN, HEADS, BLK, BLK), BF16),
        pltpu.VMEM((NB, SLOTS - WIN, HEADS, BLK, BLK), BF16),
        pltpu.VMEM((len(CROSS), HEADS, BLK, BLK), BF16),
        pltpu.VMEM(((NB + WIN - 1) * BLK, E), BF16),
        pltpu.VMEM(((NB + WIN - 1) * BLK, E), BF16),
        pltpu.VMEM((CHUNKS * BLK, E), BF16),
        pltpu.VMEM((CHUNKS,) + tile, BF16),
        pltpu.VMEM((SLOTS * BLK, E), BF16),
        pltpu.VMEM((SLOTS * BLK, E), BF16),
        pltpu.VMEM((UNROLL, 2 * BLK, SLOTS * BLK), F32),
        pltpu.VMEM((UNROLL, 2 * BLK, SLOTS * BLK), F32),
        pltpu.VMEM((UNROLL, 2 * BLK, SLOTS * BLK), BF16),
        pltpu.VMEM((UNROLL, 2 * BLK, SLOTS * BLK), BF16),
        pltpu.VMEM((E, SLOTS * BLK), F32),
        pltpu.VMEM((E, SLOTS * BLK), F32),
        pltpu.VMEM((NB, BLK), F32),
        pltpu.VMEM((NB, BLK, BLK), F32),
        pltpu.VMEM((BLK, BLK), F32),
        pltpu.VMEM((npeer + 1, NB, BLK), F32),
        pltpu.VMEM((NB + WIN - 1,) + tile, F32),
        pltpu.VMEM((NB + WIN - 1,) + tile, F32),
        pltpu.VMEM((CHUNKS * BLK, E), F32),
        pltpu.VMEM((NB, BLK, width), BF16),
        pltpu.VMEM((CHUNKS * BLK, E), BF16),
        pltpu.VMEM((CHUNKS * BLK, E), BF16),
        pltpu.VMEM((CHUNKS * BLK, E), BF16),
        pltpu.VMEM((2, WIN - 1) + tile, BF16),
        pltpu.VMEM((2, WIN - 1) + tile, BF16),
        dma((32,)),
        dma((5,)),
        dma((5,)),
        dma((2,)),
        dma((2,)),
        dma((2,)),
        dma((2,)),
        dma((1,)),
        dma((1,)),
        dma((npeer,)),
        dma((npeer,)),
        dma((NB,)),
    ]
    out = pl.pallas_call(
        functools.partial(kernel, nseq, ngrp, nhead),
        out_shape=(
            jax.ShapeDtypeStruct((NB, BLK, width), BF16),
            jax.ShapeDtypeStruct((NB, BLK, E), BF16),
            jax.ShapeDtypeStruct((NB, BLK, E), BF16),
            jax.ShapeDtypeStruct((NB, BLK), F32),
        ),
        in_specs=[hbm] * 6 + [pl.BlockSpec(memory_space=pltpu.SMEM), hbm],
        out_specs=(hbm, vmem, vmem, vmem),
        scratch_shapes=scratch,
        compiler_params=pltpu.CompilerParams(
            collective_id=0, has_side_effects=True, vmem_limit_bytes=48 * 1024 * 1024
        ),
        name="distill_backward",
    )(
        *(
            pltpu.with_memory_space_constraint(x, pltpu.HBM)
            for x in (
                queries.reshape(NB, BLK, width),
                key_rows,
                values,
                out_grad.reshape(NB, BLK, width),
                teacher_window,
                teacher_global,
            )
        ),
        global_picks.T,
        pltpu.with_memory_space_constraint(mix_weight.reshape(NB, BLK), pltpu.HBM),
    )
    query_grad, key_grad, value_grad, row_loss = out
    return (
        query_grad.reshape(NB * BLK, width),
        key_grad.reshape(NB * BLK, E),
        value_grad.reshape(NB * BLK, E),
        row_loss.reshape(NB * BLK),
    )


def solution(mesh):
    placed = (
        P("seq", ("grp", "head")),
        P("seq", ("grp", "head")),
        P("seq", ("grp", "head")),
        P("seq", ("grp", "head")),
        P("seq", None, ("grp", "head"), None, None),
        P("seq", None, ("grp", "head"), None, None),
        P("seq", None),
        P("seq"),
    )
    return jax.shard_map(
        local,
        mesh=mesh,
        in_specs=placed,
        out_specs=(
            P("seq", ("grp", "head")),
            P("seq", ("grp", "head")),
            P("seq", ("grp", "head")),
            P("seq"),
        ),
        check_vma=False,
    )
```

```python
import functools
import math

import jax
import jax.numpy as jnp
from jax import lax
from jax.experimental import pallas as pl
from jax.experimental.pallas import tpu as pltpu
from jax.sharding import PartitionSpec as P

E = 128
BLK = 128
WIN = 3
NGLOB = 4
NB = 4
HEADS = 8
SLOTS = 5
ROWS = 16
LOG2E = math.log2(math.e)
LN2 = math.log(2.0)
SCALE = 1.0 / math.sqrt(E)
NEG = -1.0e30
MESH = pl.DeviceIdType.MESH
F32 = jnp.float32
BF16 = jnp.bfloat16
CHUNKS = 2 * NGLOB
LOCAL_TILES = [(c, d) for c in range(NB) for d in range(WIN) if c + d < NB]
HALO_A = [0, 1]
HALO_B = [2, 3, 4]
UNROLL = 4
CROSS = [(3, 2), (3, 1), (2, 2)]


def ring_distance(off, nseq):
    nz = min(nseq, 8)
    ny = nseq // nz
    y, z = off // nz, off % nz
    return min(y, ny - y) + min(z, nz - z)


def kernel(
    nseq, ngrp, nhead,
    q_h, k_h, v_h, do_h, tw_h, tg_h, picks, mix_h,
    qg_h, kgrad, vgrad, loss_out,
    q_v, do_v, tw_v, tg_v, th_v, k_v, v_v, glob, glob_kv, kc, vc,
    s_scr, dp_scr, sg_scr, p_scr, dkt, dvt, mix_ref, mixc, loss_scr, lbuf,
    acc_k, acc_v, sink, qg_v, sbuf, rbuf, tsum, hs, hr,
    lsem, hsend, hrecv, bsend, brecv, rsend, rrecv, gsend, grecv, lsend, lrecv, osem,
):
    seq = lax.axis_index("seq")
    grp = lax.axis_index("grp")
    head = lax.axis_index("head")
    piece = CHUNKS * BLK // nseq
    by_distance = sorted(range(1, nseq), key=lambda off: -ring_distance(off, nseq))
    others = [lax.rem(seq + off, nseq) for off in by_distance]
    nxt, prv = lax.rem(seq + 1, nseq), lax.rem(seq + nseq - 1, nseq)

    def rows_of(dev):
        return pl.ds(pl.multiple_of(dev * piece, piece), piece)

    def total_wait(ref, sem):
        part = ref.at[pl.ds(0, (nseq - 1) * piece)]
        pltpu.make_async_copy(part, part, sem).wait()

    is_root = seq == 0

    loads = {}
    count = [0]

    def load(key, src, dst):
        copy = pltpu.make_async_copy(src, dst, lsem.at[count[0]])
        count[0] += 1
        copy.start()
        loads.setdefault(key, []).append(copy)

    load("mix", mix_h, mix_ref)
    load("kv", k_h, k_v.at[pl.ds((WIN - 1) * BLK, NB * BLK)])
    load("kv", v_h, v_v.at[pl.ds((WIN - 1) * BLK, NB * BLK)])
    for b in reversed(range(NB)):
        load(b, q_h.at[b], q_v.at[b])
        load(b, do_h.at[b], do_v.at[b])
        for c, d in LOCAL_TILES:
            if c + d == b:
                load(b, tw_h.at[c, d], tw_v.at[c, d])
        load(b, tg_h.at[b], tg_v.at[b])

    barrier = pltpu.get_barrier_semaphore()
    waits = 2
    for dev in (nxt, prv):
        pl.semaphore_signal(barrier, inc=1, device_id={"seq": dev}, device_id_type=MESH)

    @pl.when(jnp.logical_not(is_root))
    def _():
        pl.semaphore_signal(barrier, inc=1, device_id={"seq": 0}, device_id_type=MESH)

    peers = []
    for off in range(1, ngrp * nhead):
        flat = lax.rem(grp * nhead + head + off, ngrp * nhead)
        peers.append((flat // nhead, flat % nhead))
    for pg, ph in peers:
        pl.semaphore_signal(barrier, inc=1, device_id={"grp": pg, "head": ph}, device_id_type=MESH)
        waits += 1

    @pl.when(jnp.logical_not(is_root))
    def _():
        pl.semaphore_wait(barrier, waits)

    @pl.when(is_root)
    def _():
        pl.semaphore_wait(barrier, waits + nseq - 1)

    def halo_copies():
        out = []
        ends = [
            (k_h.at[pl.ds((NB - WIN + 1) * BLK, (WIN - 1) * BLK)], k_v.at[pl.ds(0, (WIN - 1) * BLK)]),
            (v_h.at[pl.ds((NB - WIN + 1) * BLK, (WIN - 1) * BLK)], v_v.at[pl.ds(0, (WIN - 1) * BLK)]),
        ] + [(tw_h.at[c, d], th_v.at[i]) for i, (c, d) in enumerate(CROSS)]
        for i, (src, dst) in enumerate(ends):
            out.append(
                pltpu.make_async_remote_copy(
                    src, dst, hsend.at[i], hrecv.at[i], device_id={"seq": nxt}, device_id_type=MESH
                )
            )
        return out

    halo = halo_copies()

    def halo_start(indices):
        @pl.when(seq < nseq - 1)
        def _():
            for i in indices:
                halo[i].start()

    @pl.when(is_root)
    def _():
        half = nseq // 2
        for dev in by_distance + [0]:
            src = (k_h if dev < half else v_h).at[pl.ds((dev % half) * piece, piece)]
            dst = glob.at[pl.ds(dev * piece, piece)]
            if dev:
                pltpu.make_async_remote_copy(
                    src, dst, bsend.at[0], brecv.at[0], device_id={"seq": dev}, device_id_type=MESH
                ).start()
            else:
                pltpu.make_async_copy(src, dst, brecv.at[0]).start()
        k_v[pl.ds(0, (WIN - 1) * BLK)] = jnp.zeros(((WIN - 1) * BLK, E), BF16)
        v_v[pl.ds(0, (WIN - 1) * BLK)] = jnp.zeros(((WIN - 1) * BLK, E), BF16)
        th_v[...] = jnp.zeros_like(th_v)

    halo_start(HALO_A)
    mine = glob.at[rows_of(seq)]
    pltpu.make_async_copy(mine, mine, brecv.at[0]).wait()
    for dev in others:
        pltpu.make_async_remote_copy(
            mine, mine, bsend.at[1], brecv.at[1], device_id={"seq": dev}, device_id_type=MESH
        ).start()
    halo_start(HALO_B)

    for copy in loads["mix"]:
        copy.wait()
    for b in range(NB):
        mixc[b] = jnp.broadcast_to(mix_ref[pl.ds(b, 1), :], (BLK, BLK)).T
    total_wait(glob, brecv.at[1])
    for n in range(CHUNKS):
        glob_kv[n] = glob[pl.ds(n * BLK, BLK), :]
    acc_k[...] = jnp.zeros_like(acc_k)
    acc_v[...] = jnp.zeros_like(acc_v)
    sink[...] = jnp.zeros_like(sink)

    for copy in loads["kv"]:
        copy.wait()

    col = lax.broadcasted_iota(jnp.int32, (ROWS, BLK), 1)
    row = lax.broadcasted_iota(jnp.int32, (ROWS, BLK), 0)
    dims_t = (((1,), (1,)), ((), ()))
    dims_c = (((0,), (0,)), ((), ()))

    def halo_wait(indices):
        @pl.when(seq > 0)
        def _():
            for i in indices:
                halo[i].wait_recv()

    def block(b):
        if b == 1:
            halo_wait([0, 1, 2])
        if b == 0:
            halo_wait([3, 4])
        for copy in loads[b]:
            copy.wait()
        for d in range(WIN):
            kc[pl.ds(d * BLK, BLK), :] = k_v[pl.ds((b + WIN - 1 - d) * BLK, BLK), :]
            vc[pl.ds(d * BLK, BLK), :] = v_v[pl.ds((b + WIN - 1 - d) * BLK, BLK), :]
        biases = [None] * SLOTS
        for d in range(1, WIN):
            if b < d:
                biases[d] = jnp.where(seq > 0, 0.0, NEG)
        for g in range(SLOTS - WIN):
            pick = picks[g, b]
            safe = jnp.maximum(pick, 0)
            kc[pl.ds((WIN + g) * BLK, BLK), :] = glob_kv[safe]
            vc[pl.ds((WIN + g) * BLK, BLK), :] = glob_kv[safe + NGLOB]
            biases[WIN + g] = jnp.where(pick >= 0, 0.0, NEG)
        tiles = []
        for d in range(WIN):
            if b >= d:
                tiles.append(tw_v.at[b - d, d])
            else:
                tiles.append(th_v.at[CROSS.index((NB + b - d, d))])
        for g in range(SLOTS - WIN):
            tiles.append(tg_v.at[b, g])
        dkt[...] = jnp.zeros_like(dkt)
        dvt[...] = jnp.zeros_like(dvt)
        loss_scr[...] = jnp.zeros_like(loss_scr)

        def operands(i):
            h0 = 2 * i
            lanes = [pl.ds(pl.multiple_of((h0 + e) * E, E), E) for e in range(2)]
            q2 = jnp.concatenate([q_v[b, :, lanes[0]], q_v[b, :, lanes[1]]], axis=0)
            do2 = jnp.concatenate([do_v[b, :, lanes[0]], do_v[b, :, lanes[1]]], axis=0)
            return lanes, q2, do2

        def forward(i, k):
            lanes, q2, do2 = operands(i)
            s_scr[k] = lax.dot_general(q2, kc[...], dims_t, preferred_element_type=F32)
            dp_scr[k] = lax.dot_general(do2, vc[...], dims_t, preferred_element_type=F32)

        def middle(i, k):
            h0 = 2 * i
            for n in range(2 * BLK // ROWS):
                e, r0 = n // (BLK // ROWS), (n % (BLK // ROWS)) * ROWS
                at = pl.ds(n * ROWS, ROWS)
                ss, ts = [], []
                for j in range(SLOTS):
                    s = s_scr[k, at, pl.ds(j * BLK, BLK)] * (SCALE * LOG2E)
                    t = tiles[j][h0 + e, pl.ds(r0, ROWS), :].astype(F32) * LOG2E
                    if j == 0:
                        live = col <= row + r0
                        s = jnp.where(live, s, NEG)
                        t = jnp.where(live, t, NEG)
                    elif biases[j] is not None:
                        s = s + biases[j]
                        t = t + biases[j]
                    ss.append(s)
                    ts.append(t)
                m_s = jnp.max(functools.reduce(jnp.maximum, ss), axis=1, keepdims=True)
                m_t = jnp.max(functools.reduce(jnp.maximum, ts), axis=1, keepdims=True)
                mix = mixc[b, pl.ds(r0, ROWS), :]
                other = (1.0 - mix) * LN2
                es, et, xs = [], [], []
                z_s = z_t = f_u = r_u = x_u = None
                for j in range(SLOTS):
                    sp = ss[j] - m_s
                    tp = ts[j] - m_t
                    e_s = jnp.exp2(sp)
                    e_t = jnp.exp2(tp)
                    u = sp - tp
                    x = other * u + dp_scr[k, at, pl.ds(j * BLK, BLK)]
                    terms = (e_s, e_t, e_t * u, e_s * u, e_s * x)
                    if j == 0:
                        z_s, z_t, f_u, r_u, x_u = terms
                    else:
                        z_s, z_t, f_u, r_u, x_u = (
                            z_s + terms[0], z_t + terms[1], f_u + terms[2], r_u + terms[3], x_u + terms[4],
                        )
                    es.append(e_s)
                    et.append(e_t)
                    xs.append(x)
                z_s, z_t, f_u, r_u, x_u = (
                    jnp.sum(v, axis=1, keepdims=True) for v in (z_s, z_t, f_u, r_u, x_u)
                )
                i_s = 1.0 / z_s
                i_t = 1.0 / z_t
                c = jnp.log(z_t) - jnp.log(z_s)
                fkl = -(f_u * i_t * LN2 + c)
                rkl = r_u * i_s * LN2 + c
                loss_scr[pl.ds(r0, ROWS), :] += mix * fkl + (1.0 - mix) * rkl
                shift = mix - x_u * i_s
                t_fac = mix * i_t
                for j in range(SLOTS):
                    p = es[j] * i_s
                    p_scr[k, at, pl.ds(j * BLK, BLK)] = p.astype(BF16)
                    sg_scr[k, at, pl.ds(j * BLK, BLK)] = (p * (xs[j] + shift) - t_fac * et[j]).astype(BF16)

        def backward(i, k):
            lanes, q2, do2 = operands(i)
            sg = sg_scr[k]
            qg = (jnp.dot(sg, kc[...], preferred_element_type=F32) * SCALE).astype(BF16)
            qg_v[b, :, lanes[0]] = qg[:BLK]
            qg_v[b, :, lanes[1]] = qg[BLK:]
            dkt[...] += lax.dot_general(q2, sg, dims_c, preferred_element_type=F32)
            dvt[...] += lax.dot_general(do2, p_scr[k], dims_c, preferred_element_type=F32)

        def pairs(step, carry):
            base = step * UNROLL
            forward(base, 0)
            for k in range(UNROLL):
                if k + 1 < UNROLL:
                    forward(base + k + 1, k + 1)
                middle(base + k, k)
                if k:
                    backward(base + k - 1, k - 1)
            backward(base + UNROLL - 1, UNROLL - 1)
            return carry

        if UNROLL == HEADS // 2:
            pairs(0, 0)
        else:
            lax.fori_loop(0, HEADS // 2 // UNROLL, pairs, 0)
        pltpu.make_async_copy(qg_v.at[b], qg_h.at[b], osem.at[b]).start()
        for d in range(WIN):
            acc_k[b + WIN - 1 - d] += dkt[:, pl.ds(d * BLK, BLK)] * SCALE
            acc_v[b + WIN - 1 - d] += dvt[:, pl.ds(d * BLK, BLK)]
        for g in range(SLOTS - WIN):
            pick = picks[g, b]
            for n in range(NGLOB):
                hit = jnp.where(pick == n, 1.0, 0.0)
                sink[pl.ds(n * BLK, BLK), :] += dkt[:, pl.ds((WIN + g) * BLK, BLK)] * (hit * SCALE)
                sink[pl.ds((NGLOB + n) * BLK, BLK), :] += dvt[:, pl.ds((WIN + g) * BLK, BLK)] * hit
        lbuf[0, pl.ds(b, 1), :] = loss_scr[...].T[0:1, :]

    for b in reversed(range(NB)):
        block(b)

    sbuf[...] = sink[...].astype(BF16)
    hs[0] = acc_k[pl.ds(0, WIN - 1)].astype(BF16)
    hs[1] = acc_v[pl.ds(0, WIN - 1)].astype(BF16)
    for n, dev in enumerate(others):
        pltpu.make_async_remote_copy(
            sbuf.at[rows_of(dev)], rbuf.at[pl.ds(n * piece, piece)], rsend.at[0], rrecv.at[0],
            device_id={"seq": dev}, device_id_type=MESH,
        ).start()

    back = pltpu.make_async_remote_copy(
        hs, hr, gsend.at[0], grecv.at[0], device_id={"seq": prv}, device_id_type=MESH
    )

    @pl.when(seq > 0)
    def _():
        back.start()

    loss_copies = []
    for n, (pg, ph) in enumerate(peers):
        copy = pltpu.make_async_remote_copy(
            lbuf.at[0], lbuf.at[n + 1], lsend.at[n], lrecv.at[n],
            device_id={"grp": pg, "head": ph}, device_id_type=MESH,
        )
        copy.start()
        loss_copies.append(copy)

    total_wait(rbuf, rrecv.at[0])
    summed = sink[rows_of(seq), :]
    for n in range(nseq - 1):
        summed = summed + rbuf[pl.ds(n * piece, piece), :].astype(F32)
    tsum[rows_of(seq), :] = summed.astype(BF16)
    give = pltpu.make_async_remote_copy(
        tsum.at[rows_of(seq)], tsum.at[rows_of(seq)], rsend.at[1], rrecv.at[1],
        device_id={"seq": 0}, device_id_type=MESH,
    )

    @pl.when(jnp.logical_not(is_root))
    def _():
        give.start()

    @pl.when(seq < nseq - 1)
    def _():
        back.wait_recv()
        acc_k[pl.ds(NB, WIN - 1)] += hr[0].astype(F32)
        acc_v[pl.ds(NB, WIN - 1)] += hr[1].astype(F32)

    total = lbuf[0]
    for n, copy in enumerate(loss_copies):
        copy.wait_recv()
        total = total + lbuf[n + 1]
    loss_out[...] = total

    @pl.when(is_root)
    def _():
        total_wait(tsum, rrecv.at[1])
        for n in range(NGLOB):
            acc_k[WIN - 1 + n] += tsum[pl.ds(n * BLK, BLK), :].astype(F32)
            acc_v[WIN - 1 + n] += tsum[pl.ds((NGLOB + n) * BLK, BLK), :].astype(F32)

    for b in range(NB):
        kgrad[b] = acc_k[b + WIN - 1].T.astype(BF16)
        vgrad[b] = acc_v[b + WIN - 1].T.astype(BF16)

    for b in range(NB):
        pltpu.make_async_copy(qg_v.at[b], qg_h.at[b], osem.at[b]).wait()
    for copy in loss_copies:
        copy.wait_send()

    @pl.when(seq > 0)
    def _():
        back.wait_send()

    @pl.when(seq < nseq - 1)
    def _():
        for copy in halo:
            copy.wait_send()

    total_wait(glob, bsend.at[1])
    total_wait(sbuf, rsend.at[0])

    @pl.when(is_root)
    def _():
        total_wait(glob, bsend.at[0])

    @pl.when(jnp.logical_not(is_root))
    def _():
        give.wait_send()


def local(queries, key_rows, values, out_grad, teacher_window, teacher_global, global_picks, mix_weight):
    nseq, ngrp, nhead = (lax.axis_size(a) for a in ("seq", "grp", "head"))
    width = HEADS * E
    hbm = pl.BlockSpec(memory_space=pltpu.HBM)
    vmem = pl.BlockSpec(memory_space=pltpu.VMEM)
    dma = pltpu.SemaphoreType.DMA
    npeer = max(ngrp * nhead - 1, 1)
    tile = (BLK, E)
    scratch = [
        pltpu.VMEM((NB, BLK, width), BF16),
        pltpu.VMEM((NB, BLK, width), BF16),
        pltpu.VMEM((NB, WIN, HEADS, BLK, BLK), BF16),
        pltpu.VMEM((NB, SLOTS - WIN, HEADS, BLK, BLK), BF16),
        pltpu.VMEM((len(CROSS), HEADS, BLK, BLK), BF16),
        pltpu.VMEM(((NB + WIN - 1) * BLK, E), BF16),
        pltpu.VMEM(((NB + WIN - 1) * BLK, E), BF16),
        pltpu.VMEM((CHUNKS * BLK, E), BF16),
        pltpu.VMEM((CHUNKS,) + tile, BF16),
        pltpu.VMEM((SLOTS * BLK, E), BF16),
        pltpu.VMEM((SLOTS * BLK, E), BF16),
        pltpu.VMEM((UNROLL, 2 * BLK, SLOTS * BLK), F32),
        pltpu.VMEM((UNROLL, 2 * BLK, SLOTS * BLK), F32),
        pltpu.VMEM((UNROLL, 2 * BLK, SLOTS * BLK), BF16),
        pltpu.VMEM((UNROLL, 2 * BLK, SLOTS * BLK), BF16),
        pltpu.VMEM((E, SLOTS * BLK), F32),
        pltpu.VMEM((E, SLOTS * BLK), F32),
        pltpu.VMEM((NB, BLK), F32),
        pltpu.VMEM((NB, BLK, BLK), F32),
        pltpu.VMEM((BLK, BLK), F32),
        pltpu.VMEM((npeer + 1, NB, BLK), F32),
        pltpu.VMEM((NB + WIN - 1,) + tile, F32),
        pltpu.VMEM((NB + WIN - 1,) + tile, F32),
        pltpu.VMEM((CHUNKS * BLK, E), F32),
        pltpu.VMEM((NB, BLK, width), BF16),
        pltpu.VMEM((CHUNKS * BLK, E), BF16),
        pltpu.VMEM((CHUNKS * BLK, E), BF16),
        pltpu.VMEM((CHUNKS * BLK, E), BF16),
        pltpu.VMEM((2, WIN - 1) + tile, BF16),
        pltpu.VMEM((2, WIN - 1) + tile, BF16),
        dma((32,)),
        dma((5,)),
        dma((5,)),
        dma((2,)),
        dma((2,)),
        dma((2,)),
        dma((2,)),
        dma((1,)),
        dma((1,)),
        dma((npeer,)),
        dma((npeer,)),
        dma((NB,)),
    ]
    out = pl.pallas_call(
        functools.partial(kernel, nseq, ngrp, nhead),
        out_shape=(
            jax.ShapeDtypeStruct((NB, BLK, width), BF16),
            jax.ShapeDtypeStruct((NB, BLK, E), BF16),
            jax.ShapeDtypeStruct((NB, BLK, E), BF16),
            jax.ShapeDtypeStruct((NB, BLK), F32),
        ),
        in_specs=[hbm] * 6 + [pl.BlockSpec(memory_space=pltpu.SMEM), hbm],
        out_specs=(hbm, vmem, vmem, vmem),
        scratch_shapes=scratch,
        compiler_params=pltpu.CompilerParams(
            collective_id=0, has_side_effects=True, vmem_limit_bytes=48 * 1024 * 1024
        ),
        name="distill_backward",
    )(
        *(
            pltpu.with_memory_space_constraint(x, pltpu.HBM)
            for x in (
                queries.reshape(NB, BLK, width),
                key_rows,
                values,
                out_grad.reshape(NB, BLK, width),
                teacher_window,
                teacher_global,
            )
        ),
        global_picks.T,
        pltpu.with_memory_space_constraint(mix_weight.reshape(NB, BLK), pltpu.HBM),
    )
    query_grad, key_grad, value_grad, row_loss = out
    return (
        query_grad.reshape(NB * BLK, width),
        key_grad.reshape(NB * BLK, E),
        value_grad.reshape(NB * BLK, E),
        row_loss.reshape(NB * BLK),
    )


def solution(mesh):
    placed = (
        P("seq", ("grp", "head")),
        P("seq", ("grp", "head")),
        P("seq", ("grp", "head")),
        P("seq", ("grp", "head")),
        P("seq", None, ("grp", "head"), None, None),
        P("seq", None, ("grp", "head"), None, None),
        P("seq", None),
        P("seq"),
    )
    return jax.shard_map(
        local,
        mesh=mesh,
        in_specs=placed,
        out_specs=(
            P("seq", ("grp", "head")),
            P("seq", ("grp", "head")),
            P("seq", ("grp", "head")),
            P("seq"),
        ),
        check_vma=False,
    )
```
